256 devices in a mesh: wide: 32 (over x, z_lo, core), narrow: 8 (over z_hi, y).
Axes of the slice: x: 4, y: 4, z: 8 (z_hi: 2, z_lo: 4; z = z_hi * 4 + z_lo), core: 2. Of those that a mesh axis runs over, the one named last changes fastest.
Arguments:
- tensor: bfloat16 [16, 8192, 8192], P(None, 'wide', 'narrow'), may hold values from -100 to 100
- first_factor: bfloat16 [16, 256], replicated, may hold values from -8 to 8
- third_factor: bfloat16 [8192, 256], P('narrow'), may hold values from -10 to 10
Outputs:
- second_factor: bfloat16 [8192, 256], P('wide')
- third_new: bfloat16 [8192, 256], P('narrow')
- first_mode: float32 [16, 256], replicated
The draws below stay inside these ranges and needn't reach their ends.
All inputs are finite; a program needn't handle non-finite values.
Results may differ from the reference program's by a relative error of at most 0.008.
Values may be sent and summed in bfloat16 or wider, within the bound.
No kernel may reach another device: no remote copies, remote signals or barrier semaphores. Data moves between devices by JAX's collectives and lax.ppermute only.
A program may use at most 128 MiB of HBM per device.

```python
import math
import jax
import jax.numpy as jnp
from jax import lax

I = 16
R = 256
J = 8192
K = 8192


def draw_tensor(key, part):
    keys = jax.random.split(jax.random.fold_in(key, 11), 4)
    noise = jnp.clip(jax.random.normal(keys[0], (I, J, K), jnp.float32), -4.0, 4.0)
    ramp_second = jnp.exp(math.log(3.0) * jnp.arange(J, dtype=jnp.float32) / J + jax.random.uniform(keys[1], (J,), jnp.float32, -0.7, 0.7)) / 1.5
    ramp_third = jnp.exp(math.log(3.0) * jnp.arange(K, dtype=jnp.float32) / K + jax.random.uniform(keys[2], (K,), jnp.float32, -0.7, 0.7)) / 1.5
    scale_first = jax.random.uniform(keys[3], (I,), jnp.float32, 0.7, 1.4)
    values = noise * scale_first[:, None, None] * ramp_second[None, :, None] * ramp_third[None, None, :]
    return values.astype(jnp.bfloat16)


def draw_first_factor(key, part):
    keys = jax.random.split(jax.random.fold_in(key, 37), 4)
    signs = jnp.where(jax.random.randint(keys[0], (I,), 0, 2) == 0, -1.0, 1.0).astype(jnp.float32)
    sizes_first = jax.random.uniform(keys[1], (I,), jnp.float32, 2.0, 3.0) * signs
    shared = jnp.exp(jax.random.uniform(keys[2], (R,), jnp.float32, math.log(0.6), math.log(1.8)))
    noise = jnp.clip(jax.random.normal(keys[3], (I, R), jnp.float32), -3.0, 3.0)
    values = sizes_first[:, None] * shared[None, :] + 0.3 * noise
    return jnp.clip(values, -8.0, 8.0).astype(jnp.bfloat16)


def draw_third_factor(key, part):
    keys = jax.random.split(jax.random.fold_in(key, 23), 3)
    common = jnp.clip(jax.random.normal(keys[1], (K,), jnp.float32), -3.0, 3.0)
    powers = 30.0 * jnp.exp(math.log(0.0001) * jnp.arange(R, dtype=jnp.float32) / (R - 1))
    mixing = jax.random.normal(keys[2], (R, R), jnp.float32) / math.sqrt(R) * jnp.sqrt(powers)[:, None]
    base = jnp.clip(jax.random.normal(keys[0], (K, R), jnp.float32), -4.0, 4.0)
    values = jnp.dot(base, mixing, precision=lax.Precision.HIGHEST) + common[:, None]
    return jnp.clip(values, -10.0, 10.0).astype(jnp.bfloat16)


def setup_inputs(seed: int = 0) -> dict:
    splits = jax.random.split(jax.random.key(seed), 4)
    return {
        "tensor": draw_tensor(jax.random.fold_in(splits[3], 71), 0),
        "first_factor": draw_first_factor(jax.random.fold_in(splits[3], 71), 0),
        "third_factor": draw_third_factor(jax.random.fold_in(splits[3], 71), 0),
    }


ridge = 0.5

def solve_rows(rows, system):
    lower = jnp.linalg.cholesky(system)
    return jax.scipy.linalg.cho_solve((lower, True), rows.T).T

def reference(tensor, first_factor, third_factor):
    first_wide = first_factor.astype(jnp.float32)
    gram_first = jnp.dot(first_factor.T.astype(jnp.float32), first_factor.astype(jnp.float32), preferred_element_type=jnp.float32) / I
    gram_third = jnp.dot(third_factor.T.astype(jnp.float32), third_factor.astype(jnp.float32), preferred_element_type=jnp.float32) / K
    identity = jnp.eye(R, dtype=jnp.float32)
    system_second = gram_first * gram_third + ridge * identity

    def accumulate(total, pieces):
        slab, coeffs = pieces
        return (total + coeffs[None, :] * jnp.dot(slab.astype(jnp.float32), third_factor.astype(jnp.float32), preferred_element_type=jnp.float32), None)
    mttkrp_second, unused = lax.scan(accumulate, jnp.zeros((J, R), jnp.float32), (tensor, first_wide))
    mttkrp_second = mttkrp_second / math.sqrt(I * K)
    second_factor = solve_rows(mttkrp_second, system_second).astype(jnp.bfloat16)
    gram_second = jnp.dot(second_factor.T.astype(jnp.float32), second_factor.astype(jnp.float32), preferred_element_type=jnp.float32) / J
    system_third = gram_first * gram_second + ridge * identity
    middle = lax.map(lambda slab: jnp.dot(slab.T.astype(jnp.float32), second_factor.astype(jnp.float32), preferred_element_type=jnp.float32), tensor)
    mttkrp_third = jnp.einsum('ikr,ir->kr', middle, first_wide, precision=lax.Precision.HIGHEST) / math.sqrt(I * J)
    third_solution = solve_rows(mttkrp_third, system_third)
    third_new = third_solution.astype(jnp.bfloat16)
    first_mode = jnp.einsum('ikr,kr->ir', middle, third_solution, precision=lax.Precision.HIGHEST) / math.sqrt(J * K)
    return (second_factor, third_new, first_mode)
```

```python
import math

import jax
import jax.numpy as jnp
from jax import lax
from jax.experimental import pallas as pl
from jax.experimental.pallas import tpu as pltpu
from jax.sharding import Mesh, PartitionSpec as P

ridge = 0.5
B = 16
WIDE = ("x", "zl", "core")
CHIP = ("x", "zl")
NARROW = ("zh", "y")
HIGHEST = lax.Precision.HIGHEST


def pieces(x):
    high = x.astype(jnp.bfloat16)
    rest = x - high.astype(jnp.float32)
    middle = rest.astype(jnp.bfloat16)
    low = (rest - middle.astype(jnp.float32)).astype(jnp.bfloat16)
    return high, middle, low


def inverse_kernel(s_ref, x_ref, m_ref, w_ref):
    n = s_ref.shape[0]
    m_ref[...] = s_ref[...]
    row = lax.broadcasted_iota(jnp.int32, (B, n), 0)
    lane = lax.broadcasted_iota(jnp.int32, (B, n), 1)
    half_row = lax.broadcasted_iota(jnp.int32, (B, 128), 0)
    whole_row = lax.broadcasted_iota(jnp.int32, (n, n), 0)
    whole_lane = lax.broadcasted_iota(jnp.int32, (n, n), 1)

    def step(k, carry):
        o = pl.multiple_of(k * B, B)
        panel = m_ref[pl.ds(o, B), :]
        front = pltpu.roll(panel, n - o, 1)
        cols = [jnp.broadcast_to(front[:, j:j + 1], (B, 128)) for j in range(B)]
        inside = (lane >= o) & (lane < o + B)
        unit = jnp.where(lane - o == row, 1.0, 0.0)
        work = jnp.where(inside, unit, panel)
        parts = [work[:, t * 128:(t + 1) * 128] for t in range(n // 128)]
        for j in range(B):
            col = cols[j]
            scale = 1.0 / col[j:j + 1, :]
            other = half_row != j
            for t in range(len(parts)):
                pivot = parts[t][j:j + 1, :] * scale
                parts[t] = jnp.where(other, parts[t] - col * pivot, pivot)
            for m in range(j + 1, B):
                pivot = cols[m][j:j + 1, :] * scale
                cols[m] = jnp.where(other, cols[m] - col * pivot, pivot)
        solved = jnp.concatenate(parts, axis=1)
        below = jnp.where(lane >= o + B, panel, 0.0)
        uh, um, ul = pieces(below)
        wh, wm, wl = pieces(solved)
        left = jnp.concatenate([uh, uh, um, uh, ul, um], axis=0)
        right = jnp.concatenate([wh, wm, wh, wl, wh, wm], axis=0)
        update = lax.dot_general(
            left, right, (((0,), (0,)), ((), ())), preferred_element_type=jnp.float32
        )
        cleared = (whole_row >= o + B) & (whole_lane >= o) & (whole_lane < o + B)
        m_ref[...] = jnp.where(cleared, 0.0, m_ref[...]) - update
        m_ref[pl.ds(o, B), :] = jnp.where(lane < o, panel, jnp.where(inside, unit, 0.0))
        w_ref[pl.ds(o, B), :] = jnp.where(lane < o + B, solved, 0.0)
        return carry

    lax.fori_loop(0, n // B, step, 0)
    x_ref[...] = lax.dot_general(
        m_ref[...], w_ref[...], (((0,), (0,)), ((), ())),
        precision=lax.Precision.HIGHEST, preferred_element_type=jnp.float32,
    )


def inverse(s):
    n = s.shape[0]
    return pl.pallas_call(
        inverse_kernel,
        out_shape=jax.ShapeDtypeStruct((n, n), jnp.float32),
        in_specs=[pl.BlockSpec(memory_space=pltpu.VMEM)],
        out_specs=pl.BlockSpec(memory_space=pltpu.VMEM),
        scratch_shapes=[pltpu.VMEM((n, n), jnp.float32), pltpu.VMEM((n, n), jnp.float32)],
        name="inverse",
    )(s)


def middle_kernel(t_ref, s_ref, f_ref, o_ref):
    i = pl.program_id(0)
    product = jnp.dot(s_ref[...], t_ref[0], preferred_element_type=jnp.float32)
    term = f_ref[0] * product

    @pl.when(i == 0)
    def _():
        o_ref[...] = term

    @pl.when(i > 0)
    def _():
        o_ref[...] += term


def third_products(tensor, second_t, first_columns):
    window, second_local, third_local = tensor.shape
    rank = second_t.shape[0]
    flops = 2 * window * second_local * third_local * rank
    return pl.pallas_call(
        middle_kernel,
        grid=(window,),
        out_shape=jax.ShapeDtypeStruct((rank, third_local), jnp.float32),
        in_specs=[
            pl.BlockSpec((1, second_local, third_local), lambda i: (i, 0, 0)),
            pl.BlockSpec((rank, second_local), lambda i: (0, 0)),
            pl.BlockSpec((1, rank, 1), lambda i: (i, 0, 0)),
        ],
        out_specs=pl.BlockSpec((rank, third_local), lambda i: (0, 0)),
        cost_estimate=pl.CostEstimate(flops=flops, bytes_accessed=tensor.size * 2, transcendentals=0),
        name="third_products",
    )(tensor, second_t, first_columns)


def first_kernel(t_ref, v_ref, s_ref, o_ref):
    product = jnp.dot(t_ref[0], v_ref[...], preferred_element_type=jnp.float32)
    o_ref[0] = jnp.sum(product * s_ref[...], axis=0, keepdims=True)


def first_products(tensor, third_new, second_wide):
    window, second_local, third_local = tensor.shape
    rank = third_new.shape[1]
    flops = 2 * window * second_local * third_local * rank
    out = pl.pallas_call(
        first_kernel,
        grid=(window,),
        out_shape=jax.ShapeDtypeStruct((window, 1, rank), jnp.float32),
        in_specs=[
            pl.BlockSpec((1, second_local, third_local), lambda i: (i, 0, 0)),
            pl.BlockSpec((third_local, rank), lambda i: (0, 0)),
            pl.BlockSpec((second_local, rank), lambda i: (0, 0)),
        ],
        out_specs=pl.BlockSpec((1, 1, rank), lambda i: (i, 0, 0)),
        cost_estimate=pl.CostEstimate(flops=flops, bytes_accessed=tensor.size * 2, transcendentals=0),
        name="first_products",
    )(tensor, third_new, second_wide)
    return out.reshape(window, rank)


def exchange(x, axes):
    return lax.all_to_all(x, axes, 0, 0, tiled=True)


def scatter_sum(x, axes):
    n = lax.axis_size(axes)
    return jnp.sum(exchange(x.reshape(n, x.shape[0] // n, x.shape[1]), axes), axis=0)


def gather(x, axes):
    n = lax.axis_size(axes)
    return exchange(jnp.broadcast_to(x[None], (n,) + x.shape), axes).reshape(n * x.shape[0], x.shape[1])


def gather_sum(x, axes):
    n = lax.axis_size(axes)
    return jnp.sum(exchange(jnp.broadcast_to(x[None], (n,) + x.shape), axes), axis=0)


def swap(x):
    return lax.ppermute(x, "core", [(0, 1), (1, 0)])


def on_device(tensor, first_factor, third_factor):
    window, second_local, third_local = tensor.shape
    rank = first_factor.shape[1]
    second_total = second_local * lax.axis_size(WIDE)
    third_total = third_local * lax.axis_size(NARROW)
    core = lax.axis_index("core")
    first_wide = first_factor.astype(jnp.float32)
    identity = jnp.eye(rank, dtype=jnp.float32)
    gram_first = jnp.dot(first_factor.T, first_factor, preferred_element_type=jnp.float32) / window

    gram_part = jnp.dot(third_factor.T, third_factor, preferred_element_type=jnp.float32)
    gram_third = gather(scatter_sum(gram_part, NARROW), NARROW) / third_total
    inverse_second = inverse(gram_first * gram_third + ridge * identity)

    contracted = jnp.dot(
        tensor.reshape(window * second_local, third_local),
        third_factor,
        preferred_element_type=jnp.float32,
    ).reshape(window, second_local, rank)
    partial_second = jnp.einsum(
        "ijr,ir->jr", contracted, first_wide, precision=HIGHEST
    ) / math.sqrt(window * third_total)
    mttkrp_second = gather(scatter_sum(partial_second, NARROW), NARROW)
    second_factor = jnp.dot(mttkrp_second, inverse_second, precision=HIGHEST).astype(jnp.bfloat16)

    gram_local = jnp.dot(second_factor.T, second_factor, preferred_element_type=jnp.float32)
    gram_second = gather(scatter_sum(gram_local, WIDE), WIDE) / second_total
    inverse_third = inverse(gram_first * gram_second + ridge * identity)

    partial_third = third_products(tensor, second_factor.T, first_wide[:, :, None])
    partial_third = partial_third / math.sqrt(window * second_total)
    halves = partial_third.reshape(2, rank // 2, third_local)
    mine = jnp.where(core == 0, halves[0], halves[1])
    other = jnp.where(core == 0, halves[1], halves[0])
    mine = mine + swap(other)
    mine = gather(scatter_sum(mine, CHIP), CHIP)
    theirs = swap(mine)
    mttkrp_third = jnp.where(
        core == 0, jnp.concatenate([mine, theirs], 0), jnp.concatenate([theirs, mine], 0)
    )
    third_solution = jnp.dot(inverse_third, mttkrp_third, precision=HIGHEST)
    third_new = third_solution.astype(jnp.bfloat16).T

    partial_first = first_products(tensor, third_new, second_factor.astype(jnp.float32))
    partial_first = partial_first / math.sqrt(second_total * third_total)
    partial_first = partial_first + swap(partial_first)
    first_mode = gather_sum(gather_sum(partial_first, CHIP), NARROW)
    return (second_factor, third_new, first_mode)


def solution(mesh):
    fine = Mesh(mesh.devices.reshape(4, 4, 2, 2, 4), WIDE + NARROW)
    in_specs = (P(None, WIDE, NARROW), P(), P(NARROW, None))
    out_specs = (P(WIDE, None), P(NARROW, None), P())
    return jax.shard_map(
        on_device, mesh=fine, in_specs=in_specs, out_specs=out_specs, check_vma=False
    )
```

```python
import functools
import math

import jax
import jax.numpy as jnp
from jax import lax
from jax.experimental import pallas as pl
from jax.experimental.pallas import tpu as pltpu
from jax.sharding import Mesh, PartitionSpec as P

ridge = 0.5
B = 16
WIDE = ("x", "zl", "core")
CHIP = ("x", "zl")
NARROW = ("zh", "y")
HIGHEST = lax.Precision.HIGHEST


def pieces(x):
    high = x.astype(jnp.bfloat16)
    rest = x - high.astype(jnp.float32)
    middle = rest.astype(jnp.bfloat16)
    low = (rest - middle.astype(jnp.float32)).astype(jnp.bfloat16)
    return high, middle, low


def inverse_kernel(places, total, *refs):
    part_refs, (f_ref, x_ref, m_ref, w_ref) = refs[:-4], refs[-4:]
    n = f_ref.shape[0]
    depth = part_refs[0].shape[0]
    for place, part_ref in zip(places(), part_refs):
        base = pl.multiple_of(place * depth, depth)
        here = (depth, n)
        diagonal = lax.broadcasted_iota(jnp.int32, here, 0) + base == lax.broadcasted_iota(jnp.int32, here, 1)
        m_ref[pl.ds(base, depth), :] = f_ref[pl.ds(base, depth), :] * (
            part_ref[...] * (1.0 / total)
        ) + jnp.where(diagonal, ridge, 0.0)
    row = lax.broadcasted_iota(jnp.int32, (B, n), 0)
    lane = lax.broadcasted_iota(jnp.int32, (B, n), 1)
    half_row = lax.broadcasted_iota(jnp.int32, (B, 128), 0)
    whole_row = lax.broadcasted_iota(jnp.int32, (n, n), 0)
    whole_lane = lax.broadcasted_iota(jnp.int32, (n, n), 1)

    def step(k, carry):
        o = pl.multiple_of(k * B, B)
        panel = m_ref[pl.ds(o, B), :]
        front = pltpu.roll(panel, n - o, 1)
        cols = [jnp.broadcast_to(front[:, j:j + 1], (B, 128)) for j in range(B)]
        inside = (lane >= o) & (lane < o + B)
        unit = jnp.where(lane - o == row, 1.0, 0.0)
        work = jnp.where(inside, unit, panel)
        parts = [work[:, t * 128:(t + 1) * 128] for t in range(n // 128)]
        for j in range(B):
            col = cols[j]
            scale = 1.0 / col[j:j + 1, :]
            other = half_row != j
            for t in range(len(parts)):
                pivot = parts[t][j:j + 1, :] * scale
                parts[t] = jnp.where(other, parts[t] - col * pivot, pivot)
            for m in range(j + 1, B):
                pivot = cols[m][j:j + 1, :] * scale
                cols[m] = jnp.where(other, cols[m] - col * pivot, pivot)
        solved = jnp.concatenate(parts, axis=1)
        below = jnp.where(lane >= o + B, panel, 0.0)
        uh, um, ul = pieces(below)
        wh, wm, wl = pieces(solved)
        left = jnp.concatenate([uh, uh, um, uh, ul, um], axis=0)
        right = jnp.concatenate([wh, wm, wh, wl, wh, wm], axis=0)
        update = lax.dot_general(
            left, right, (((0,), (0,)), ((), ())), preferred_element_type=jnp.float32
        )
        cleared = (whole_row >= o + B) & (whole_lane >= o) & (whole_lane < o + B)
        m_ref[...] = jnp.where(cleared, 0.0, m_ref[...]) - update
        m_ref[pl.ds(o, B), :] = jnp.where(lane < o, panel, jnp.where(inside, unit, 0.0))
        w_ref[pl.ds(o, B), :] = jnp.where(lane < o + B, solved, 0.0)
        return carry

    lax.fori_loop(0, n // B, step, 0)
    x_ref[...] = lax.dot_general(
        m_ref[...], w_ref[...], (((0,), (0,)), ((), ())),
        precision=lax.Precision.HIGHEST, preferred_element_type=jnp.float32,
    )


def inverse(parts, places, gram_first, total):
    n = gram_first.shape[0]
    return pl.pallas_call(
        functools.partial(inverse_kernel, places, total),
        out_shape=jax.ShapeDtypeStruct((n, n), jnp.float32),
        in_specs=[pl.BlockSpec(memory_space=pltpu.VMEM)] * (len(parts) + 1),
        out_specs=pl.BlockSpec(memory_space=pltpu.VMEM),
        scratch_shapes=[pltpu.VMEM((n, n), jnp.float32), pltpu.VMEM((n, n), jnp.float32)],
        cost_estimate=pl.CostEstimate(flops=6 * 2 * n**3, bytes_accessed=8 * n * n, transcendentals=0),
        compiler_params=pltpu.CompilerParams(vmem_limit_bytes=8 << 20),
        name="inverse",
    )(*parts, gram_first)


def exchange(x, axes):
    return lax.all_to_all(x, axes, 0, 0, tiled=True)


def scatter_sum(x, axes):
    n = lax.axis_size(axes)
    return jnp.sum(exchange(x.reshape(n, x.shape[0] // n, x.shape[1]), axes), axis=0)


def gather(x, axes):
    n = lax.axis_size(axes)
    return exchange(jnp.broadcast_to(x[None], (n,) + x.shape), axes).reshape(n * x.shape[0], x.shape[1])


def shift(x, axis, d):
    n = lax.axis_size(axis)
    return lax.ppermute(x, axis, [(s, (s + d) % n) for s in range(n)])


def ring_scatter(x, axis):
    n = lax.axis_size(axis)
    me = lax.axis_index(axis)
    blocks = x.reshape(n, x.shape[0] // n, x.shape[1])
    take = lambda d: lax.dynamic_index_in_dim(blocks, lax.rem(me + d, n), 0, keepdims=False)
    arrived = [shift(take(d), axis, d) for d in range(1, n)]
    return sum(arrived, take(0))


def ring_sum(x, axis):
    return sum([shift(x, axis, d) for d in range(1, lax.axis_size(axis))], x)


def ring_gather(x, axis):
    return [x] + [shift(x, axis, d) for d in range(1, lax.axis_size(axis))]


def keep(x, bit):
    half = x.shape[0] // 2
    low, high = x[:half], x[half:]
    return jnp.where(bit == 0, low, high), jnp.where(bit == 0, high, low)


def join(mine, theirs, bit):
    return jnp.where(
        bit == 0, jnp.concatenate([mine, theirs], 0), jnp.concatenate([theirs, mine], 0)
    )


def narrow_places():
    me = lax.axis_index("y")
    return [lax.rem(me + 4 - d, 4) for d in range(4)]


def wide_places():
    me = lax.axis_index("x")
    core = lax.axis_index("core")
    ring = [lax.rem(me + 4 - d, 4) for d in range(4)]
    return [core * 4 + r for r in ring] + [(1 - core) * 4 + r for r in ring]


def on_device(tensor, first_factor, third_factor):
    window, second_local, third_local = tensor.shape
    second_total = second_local * lax.axis_size(WIDE)
    third_total = third_local * lax.axis_size(NARROW)
    core = lax.axis_index("core")
    first_wide = first_factor.astype(jnp.float32)
    first_second = first_wide / math.sqrt(window * third_total)
    first_third = first_wide / math.sqrt(window * second_total)
    gram_first = jnp.dot(first_factor.T, first_factor, preferred_element_type=jnp.float32) / window

    gram_part = jnp.dot(third_factor.T, third_factor, preferred_element_type=jnp.float32)
    gram_part = ring_scatter(gram_part, "y")
    gram_part = ring_sum(gram_part, "zh")
    parts = ring_gather(gram_part, "y")
    inverse_second = inverse(parts, narrow_places, gram_first, third_total)

    contracted = jnp.einsum("ijk,kr->ijr", tensor, third_factor, preferred_element_type=jnp.float32)
    partial_second = jnp.einsum(
        "ijr,ir->jr", contracted, first_second, precision=HIGHEST
    )
    row = scatter_sum(partial_second, NARROW)
    mttkrp_second = gather(row, NARROW)
    second_factor = jnp.dot(mttkrp_second, inverse_second, precision=HIGHEST).astype(jnp.bfloat16)

    gram_local = jnp.dot(second_factor.T, second_factor, preferred_element_type=jnp.float32)
    mine, other = keep(gram_local, core)
    mine = mine + shift(other, "core", 1)
    mine = ring_scatter(mine, "x")
    mine = ring_sum(mine, "zl")
    parts = ring_gather(mine, "x")
    parts = parts + [shift(part, "core", 1) for part in parts]
    inverse_third = inverse(parts, wide_places, gram_first, second_total)

    middle = jnp.einsum("ijk,jr->ikr", tensor, second_factor, preferred_element_type=jnp.float32)
    partial_third = jnp.einsum(
        "ikr,ir->kr", middle, first_third, precision=HIGHEST
    )
    mine, other = keep(partial_third, core)
    mine = mine + shift(other, "core", 1)
    mttkrp_third = scatter_sum(mine, CHIP)
    third_solution = jnp.dot(mttkrp_third, inverse_third, precision=HIGHEST)
    mine = gather(third_solution.astype(jnp.bfloat16), CHIP)
    third_new = join(mine, shift(mine, "core", 1), core)

    back = jnp.einsum("ijk,kr->ijr", tensor, third_new, preferred_element_type=jnp.float32)
    partial_first = jnp.einsum(
        "ijr,jr->ir", back, second_factor.astype(jnp.float32), precision=HIGHEST
    )
    partial_first = partial_first + shift(partial_first, "core", 1)
    partial_first = ring_sum(partial_first, "x").astype(jnp.bfloat16)
    axes = ("zl",) + NARROW
    n = lax.axis_size(axes)
    copies = jnp.broadcast_to(partial_first[None], (n,) + partial_first.shape)
    first_mode = jnp.sum(exchange(copies, axes), axis=0, dtype=jnp.float32)
    first_mode = first_mode / math.sqrt(second_total * third_total)
    return (second_factor, third_new, first_mode)


def solution(mesh):
    fine = Mesh(mesh.devices.reshape(4, 4, 2, 2, 4), WIDE + NARROW)
    in_specs = (P(None, WIDE, NARROW), P(), P(NARROW, None))
    out_specs = (P(WIDE, None), P(NARROW, None), P())
    return jax.shard_map(
        on_device, mesh=fine, in_specs=in_specs, out_specs=out_specs, check_vma=False
    )
```

```python
import functools
import math

import jax
import jax.numpy as jnp
from jax import lax
from jax.experimental import pallas as pl
from jax.experimental.pallas import tpu as pltpu
from jax.sharding import Mesh, PartitionSpec as P

ridge = 0.5
B = 16
WIDE = ("x", "zl", "core")
CHIP = ("x", "zl")
NARROW = ("zh", "y")
HIGHEST = lax.Precision.HIGHEST


def pieces(x):
    high = x.astype(jnp.bfloat16)
    rest = x - high.astype(jnp.float32)
    middle = rest.astype(jnp.bfloat16)
    low = (rest - middle.astype(jnp.float32)).astype(jnp.bfloat16)
    return high, middle, low


def split_pair(a, b):
    ah, am, al = pieces(a)
    bh, bm, bl = pieces(b)
    left = jnp.concatenate([ah, ah, am, ah, al, am], axis=0)
    return left, jnp.concatenate([bh, bm, bh, bl, bh, bm], axis=0)


def cross(a, b, **kw):
    return lax.dot_general(
        a, b, (((0,), (0,)), ((), ())), preferred_element_type=jnp.float32, **kw
    )


def inverse_kernel(places, total, *refs):
    part_refs, (f_ref, x_ref, m_ref, w_ref) = refs[:-4], refs[-4:]
    n = f_ref.shape[0]
    depth = part_refs[0].shape[0]
    for place, part_ref in zip(places(), part_refs):
        base = pl.multiple_of(place * depth, depth)
        here = (depth, n)
        diagonal = lax.broadcasted_iota(jnp.int32, here, 0) + base == lax.broadcasted_iota(jnp.int32, here, 1)
        m_ref[pl.ds(base, depth), :] = f_ref[pl.ds(base, depth), :] * (
            part_ref[...] * (1.0 / total)
        ) + jnp.where(diagonal, ridge, 0.0)
    row = lax.broadcasted_iota(jnp.int32, (B, n), 0)
    lane = lax.broadcasted_iota(jnp.int32, (B, n), 1)
    half_row = lax.broadcasted_iota(jnp.int32, (B, 128), 0)
    whole_row = lax.broadcasted_iota(jnp.int32, (n, n), 0)
    whole_lane = lax.broadcasted_iota(jnp.int32, (n, n), 1)

    def step(k, carry):
        panel, left, right = carry
        o = pl.multiple_of(k * B, B)
        cleared = (whole_row >= o) & (whole_lane >= o - B) & (whole_lane < o)
        m_ref[...] = jnp.where(cleared, 0.0, m_ref[...]) - cross(left, right)
        front = pltpu.roll(panel, n - o, 1)
        cols = [jnp.broadcast_to(front[:, j:j + 1], (B, 128)) for j in range(B)]
        inside = (lane >= o) & (lane < o + B)
        unit = jnp.where(lane - o == row, 1.0, 0.0)
        work = jnp.where(inside, unit, panel)
        parts = [work[:, t * 128:(t + 1) * 128] for t in range(n // 128)]
        for j in range(B):
            col = cols[j]
            scale = 1.0 / col[j:j + 1, :]
            other = half_row != j
            for t in range(len(parts)):
                pivot = parts[t][j:j + 1, :] * scale
                parts[t] = jnp.where(other, parts[t] - col * pivot, pivot)
            for m in range(j + 1, B):
                pivot = cols[m][j:j + 1, :] * scale
                cols[m] = jnp.where(other, cols[m] - col * pivot, pivot)
        solved = jnp.concatenate(parts, axis=1)
        left, right = split_pair(jnp.where(lane >= o + B, panel, 0.0), solved)
        ahead = split_pair(front[:, :128], front[:, :128])[0][:, B:2 * B]
        following = pl.multiple_of(jnp.minimum(o + B, n - B), B)
        panel_next = jnp.where(inside, 0.0, m_ref[pl.ds(following, B), :]) - cross(ahead, right)
        m_ref[pl.ds(o, B), :] = jnp.where(lane < o, panel, jnp.where(inside, unit, 0.0))
        w_ref[pl.ds(o, B), :] = jnp.where(lane < o + B, solved, 0.0)
        return panel_next, left, right

    nothing = jnp.zeros((6 * B, n), jnp.bfloat16)
    lax.fori_loop(0, n // B, step, (m_ref[0:B, :], nothing, nothing))
    x_ref[...] = cross(m_ref[...], w_ref[...], precision=HIGHEST)


def inverse(parts, places, gram_first, total):
    n = gram_first.shape[0]
    return pl.pallas_call(
        functools.partial(inverse_kernel, places, total),
        out_shape=jax.ShapeDtypeStruct((n, n), jnp.float32),
        in_specs=[pl.BlockSpec(memory_space=pltpu.VMEM)] * (len(parts) + 1),
        out_specs=pl.BlockSpec(memory_space=pltpu.VMEM),
        scratch_shapes=[pltpu.VMEM((n, n), jnp.float32), pltpu.VMEM((n, n), jnp.float32)],
        cost_estimate=pl.CostEstimate(flops=6 * 2 * n**3, bytes_accessed=8 * n * n, transcendentals=0),
        compiler_params=pltpu.CompilerParams(vmem_limit_bytes=8 << 20),
        name="inverse",
    )(*parts, gram_first)


def exchange(x, axes):
    return lax.all_to_all(x, axes, 0, 0, tiled=True)


def scatter_sum(x, axes):
    n = lax.axis_size(axes)
    return jnp.sum(exchange(x.reshape(n, x.shape[0] // n, x.shape[1]), axes), axis=0)


def gather(x, axes):
    n = lax.axis_size(axes)
    return exchange(jnp.broadcast_to(x[None], (n,) + x.shape), axes).reshape(n * x.shape[0], x.shape[1])


def shift(x, axis, d):
    n = lax.axis_size(axis)
    return lax.ppermute(x, axis, [(s, (s + d) % n) for s in range(n)])


def ring_scatter(x, axis):
    n = lax.axis_size(axis)
    me = lax.axis_index(axis)
    blocks = x.reshape(n, x.shape[0] // n, x.shape[1])
    take = lambda d: lax.dynamic_index_in_dim(blocks, lax.rem(me + d, n), 0, keepdims=False)
    arrived = [shift(take(d), axis, d) for d in range(1, n)]
    return sum(arrived, take(0))


def ring_sum(x, axis):
    return sum([shift(x, axis, d) for d in range(1, lax.axis_size(axis))], x)


def ring_gather(x, axis):
    return [x] + [shift(x, axis, d) for d in range(1, lax.axis_size(axis))]


def pair(x, axis, d):
    return lax.ppermute(x, axis, [(s, s ^ d) for s in range(lax.axis_size(axis))])


def quad_gather(x, axis):
    return [x] + [pair(x, axis, d) for d in (1, 2, 3)]


def ordered(parts, me):
    odd = lax.rem(me, 2) == 1
    low = [jnp.where(odd, parts[1], parts[0]), jnp.where(odd, parts[0], parts[1])]
    high = [jnp.where(odd, parts[3], parts[2]), jnp.where(odd, parts[2], parts[3])]
    up = me >= 2
    first = [jnp.where(up, h, l) for l, h in zip(low, high)]
    last = [jnp.where(up, l, h) for l, h in zip(low, high)]
    return jnp.concatenate(first + last, axis=0)


def keep(x, bit):
    half = x.shape[0] // 2
    low, high = x[:half], x[half:]
    return jnp.where(bit == 0, low, high), jnp.where(bit == 0, high, low)


def join(mine, theirs, bit):
    return jnp.where(
        bit == 0, jnp.concatenate([mine, theirs], 0), jnp.concatenate([theirs, mine], 0)
    )


def narrow_places():
    me = lax.axis_index("y")
    return [lax.rem(me + 4 - d, 4) for d in range(4)]


def wide_places():
    me = lax.axis_index("x")
    core = lax.axis_index("core")
    ring = [lax.rem(me + 4 - d, 4) for d in range(4)]
    return [core * 4 + r for r in ring] + [(1 - core) * 4 + r for r in ring]


def on_device(tensor, first_factor, third_factor):
    window, second_local, third_local = tensor.shape
    second_total = second_local * lax.axis_size(WIDE)
    third_total = third_local * lax.axis_size(NARROW)
    core = lax.axis_index("core")
    first_wide = first_factor.astype(jnp.float32)
    first_second = first_wide / math.sqrt(window * third_total)
    first_third = first_wide / math.sqrt(window * second_total)
    gram_first = jnp.dot(first_factor.T, first_factor, preferred_element_type=jnp.float32) / window

    gram_part = jnp.dot(third_factor.T, third_factor, preferred_element_type=jnp.float32)
    gram_part = ring_scatter(gram_part, "y")
    gram_part = ring_sum(gram_part, "zh")
    parts = ring_gather(gram_part, "y")
    inverse_second = inverse(parts, narrow_places, gram_first, third_total)

    contracted = jnp.einsum("ijk,kr->ijr", tensor, third_factor, preferred_element_type=jnp.float32)
    partial_second = jnp.einsum(
        "ijr,ir->jr", contracted, first_second, precision=HIGHEST
    )
    row = scatter_sum(partial_second, NARROW)
    mttkrp_second = gather(row, NARROW)
    second_factor = jnp.dot(mttkrp_second, inverse_second, precision=HIGHEST).astype(jnp.bfloat16)

    gram_local = jnp.dot(second_factor.T, second_factor, preferred_element_type=jnp.float32)
    mine, other = keep(gram_local, core)
    mine = mine + shift(other, "core", 1)
    mine = ring_scatter(mine, "x")
    mine = ring_sum(mine, "zl")
    parts = ring_gather(mine, "x")
    parts = parts + [shift(part, "core", 1) for part in parts]
    inverse_third = inverse(parts, wide_places, gram_first, second_total)

    middle = jnp.einsum("ijk,jr->ikr", tensor, second_factor, preferred_element_type=jnp.float32)
    partial_third = jnp.einsum(
        "ikr,ir->kr", middle, first_third, precision=HIGHEST
    )
    mine, other = keep(partial_third, core)
    mine = mine + shift(other, "core", 1)
    mttkrp_third = scatter_sum(mine, CHIP)
    third_solution = jnp.dot(mttkrp_third, inverse_third, precision=HIGHEST)
    parts = quad_gather(third_solution.astype(jnp.bfloat16), "zl")
    block = ordered(parts, lax.axis_index("zl"))
    parts = quad_gather(block, "x")
    mine = ordered(parts, lax.axis_index("x"))
    third_new = join(mine, shift(mine, "core", 1), core)

    back = jnp.einsum("ijk,kr->ijr", tensor, third_new, preferred_element_type=jnp.float32)
    partial_first = jnp.einsum(
        "ijr,jr->ir", back, second_factor.astype(jnp.float32), precision=HIGHEST
    )
    partial_first = partial_first + shift(partial_first, "core", 1)
    scale = 1.0 / math.sqrt(second_total * third_total)
    partial_first = (ring_sum(partial_first, "x") * scale).astype(jnp.bfloat16)
    axes = ("zl",) + NARROW
    n = lax.axis_size(axes)
    copies = jnp.broadcast_to(partial_first[None], (n,) + partial_first.shape)
    first_mode = jnp.sum(exchange(copies, axes), axis=0, dtype=jnp.float32)
    return (second_factor, third_new, first_mode)


def solution(mesh):
    fine = Mesh(mesh.devices.reshape(4, 4, 2, 2, 4), WIDE + NARROW)
    in_specs = (P(None, WIDE, NARROW), P(), P(NARROW, None))
    out_specs = (P(WIDE, None), P(NARROW, None), P())
    return jax.shard_map(
        on_device, mesh=fine, in_specs=in_specs, out_specs=out_specs, check_vma=False
    )
```

```python
import functools
import math

import jax
import jax.numpy as jnp
from jax import lax
from jax.experimental import pallas as pl
from jax.experimental.pallas import tpu as pltpu
from jax.sharding import Mesh, PartitionSpec as P

ridge = 0.5
B = 16
WIDE = ("x", "zl", "core")
CHIP = ("x", "zl")
NARROW = ("zh", "y")
HIGHEST = lax.Precision.HIGHEST


def pieces(x):
    high = x.astype(jnp.bfloat16)
    rest = x - high.astype(jnp.float32)
    middle = rest.astype(jnp.bfloat16)
    low = (rest - middle.astype(jnp.float32)).astype(jnp.bfloat16)
    return high, middle, low


def split_pair(a, b):
    ah, am, al = pieces(a)
    bh, bm, bl = pieces(b)
    left = jnp.concatenate([ah, ah, am, ah, al, am], axis=0)
    return left, jnp.concatenate([bh, bm, bh, bl, bh, bm], axis=0)


def cross(a, b, **kw):
    return lax.dot_general(
        a, b, (((0,), (0,)), ((), ())), preferred_element_type=jnp.float32, **kw
    )


def inverse_kernel(places, total, *refs):
    part_refs, (f_ref, x_ref, m_ref, w_ref) = refs[:-4], refs[-4:]
    n = f_ref.shape[0]
    depth = part_refs[0].shape[0]
    for place, part_ref in zip(places(), part_refs):
        base = pl.multiple_of(place * depth, depth)
        here = (depth, n)
        diagonal = lax.broadcasted_iota(jnp.int32, here, 0) + base == lax.broadcasted_iota(jnp.int32, here, 1)
        m_ref[pl.ds(base, depth), :] = f_ref[pl.ds(base, depth), :] * (
            part_ref[...] * (1.0 / total)
        ) + jnp.where(diagonal, ridge, 0.0)
    row = lax.broadcasted_iota(jnp.int32, (B, n), 0)
    lane = lax.broadcasted_iota(jnp.int32, (B, n), 1)
    half_row = lax.broadcasted_iota(jnp.int32, (B, 128), 0)
    whole_row = lax.broadcasted_iota(jnp.int32, (n, n), 0)
    whole_lane = lax.broadcasted_iota(jnp.int32, (n, n), 1)

    def step(k, carry):
        panel, left, right = carry
        o = pl.multiple_of(k * B, B)
        cleared = (whole_row >= o) & (whole_lane >= o - B) & (whole_lane < o)
        m_ref[...] = jnp.where(cleared, 0.0, m_ref[...]) - cross(left, right)
        front = pltpu.roll(panel, n - o, 1)
        cols = [jnp.broadcast_to(front[:, j:j + 1], (B, 128)) for j in range(B)]
        inside = (lane >= o) & (lane < o + B)
        unit = jnp.where(lane - o == row, 1.0, 0.0)
        work = jnp.where(inside, unit, panel)
        parts = [work[:, t * 128:(t + 1) * 128] for t in range(n // 128)]
        for j in range(B):
            col = cols[j]
            scale = 1.0 / col[j:j + 1, :]
            other = half_row != j
            for t in range(len(parts)):
                pivot = parts[t][j:j + 1, :] * scale
                parts[t] = jnp.where(other, parts[t] - col * pivot, pivot)
            for m in range(j + 1, B):
                pivot = cols[m][j:j + 1, :] * scale
                cols[m] = jnp.where(other, cols[m] - col * pivot, pivot)
        solved = jnp.concatenate(parts, axis=1)
        left, right = split_pair(jnp.where(lane >= o + B, panel, 0.0), solved)
        ahead = split_pair(front[:, :128], front[:, :128])[0][:, B:2 * B]
        following = pl.multiple_of(jnp.minimum(o + B, n - B), B)
        panel_next = jnp.where(inside, 0.0, m_ref[pl.ds(following, B), :]) - cross(ahead, right)
        m_ref[pl.ds(o, B), :] = jnp.where(lane < o, panel, jnp.where(inside, unit, 0.0))
        w_ref[pl.ds(o, B), :] = jnp.where(lane < o + B, solved, 0.0)
        return panel_next, left, right

    nothing = jnp.zeros((6 * B, n), jnp.bfloat16)
    lax.fori_loop(0, n // B, step, (m_ref[0:B, :], nothing, nothing))
    x_ref[...] = cross(m_ref[...], w_ref[...], precision=HIGHEST)


def inverse(parts, places, gram_first, total):
    n = gram_first.shape[0]
    return pl.pallas_call(
        functools.partial(inverse_kernel, places, total),
        out_shape=jax.ShapeDtypeStruct((n, n), jnp.float32),
        in_specs=[pl.BlockSpec(memory_space=pltpu.VMEM)] * (len(parts) + 1),
        out_specs=pl.BlockSpec(memory_space=pltpu.VMEM),
        scratch_shapes=[pltpu.VMEM((n, n), jnp.float32), pltpu.VMEM((n, n), jnp.float32)],
        cost_estimate=pl.CostEstimate(flops=6 * 2 * n**3, bytes_accessed=8 * n * n, transcendentals=0),
        compiler_params=pltpu.CompilerParams(vmem_limit_bytes=8 << 20),
        name="inverse",
    )(*parts, gram_first)


def exchange(x, axes):
    return lax.all_to_all(x, axes, 0, 0, tiled=True)


def scatter_sum(x, axes):
    n = lax.axis_size(axes)
    return jnp.sum(exchange(x.reshape(n, x.shape[0] // n, x.shape[1]), axes), axis=0)


def gather(x, axes):
    n = lax.axis_size(axes)
    return exchange(jnp.broadcast_to(x[None], (n,) + x.shape), axes).reshape(n * x.shape[0], x.shape[1])


def shift(x, axis, d):
    n = lax.axis_size(axis)
    return lax.ppermute(x, axis, [(s, (s + d) % n) for s in range(n)])


def ring_scatter(x, axis):
    n = lax.axis_size(axis)
    me = lax.axis_index(axis)
    blocks = x.reshape(n, x.shape[0] // n, x.shape[1])
    take = lambda d: lax.dynamic_index_in_dim(blocks, lax.rem(me + d, n), 0, keepdims=False)
    arrived = [shift(take(d), axis, d) for d in range(1, n)]
    return sum(arrived, take(0))


def ring_sum(x, axis):
    return sum([shift(x, axis, d) for d in range(1, lax.axis_size(axis))], x)


def ring_gather(x, axis):
    return [x] + [shift(x, axis, d) for d in range(1, lax.axis_size(axis))]


def pair(x, axis, d):
    return lax.ppermute(x, axis, [(s, s ^ d) for s in range(lax.axis_size(axis))])


def quad_gather(x, axis):
    return [x] + [pair(x, axis, d) for d in (1, 2, 3)]


def ordered(parts, me):
    odd = lax.rem(me, 2) == 1
    low = [jnp.where(odd, parts[1], parts[0]), jnp.where(odd, parts[0], parts[1])]
    high = [jnp.where(odd, parts[3], parts[2]), jnp.where(odd, parts[2], parts[3])]
    up = me >= 2
    first = [jnp.where(up, h, l) for l, h in zip(low, high)]
    last = [jnp.where(up, l, h) for l, h in zip(low, high)]
    return jnp.concatenate(first + last, axis=0)


def keep(x, bit):
    half = x.shape[0] // 2
    low, high = x[:half], x[half:]
    return jnp.where(bit == 0, low, high), jnp.where(bit == 0, high, low)


def join(mine, theirs, bit):
    return jnp.where(
        bit == 0, jnp.concatenate([mine, theirs], 0), jnp.concatenate([theirs, mine], 0)
    )


def quad_places():
    me = lax.axis_index("x")
    odd = lax.rem(me, 2)
    return [me, me + 1 - 2 * odd, lax.rem(me + 2, 4), 3 - me]


def ring_places():
    me = lax.axis_index("y")
    return [lax.rem(me + 4 - d, 4) for d in range(4)]


def on_device(tensor, first_factor, third_factor):
    window, second_local, third_local = tensor.shape
    second_total = second_local * lax.axis_size(WIDE)
    third_total = third_local * lax.axis_size(NARROW)
    core = lax.axis_index("core")
    first_wide = first_factor.astype(jnp.float32)
    first_second = first_wide / math.sqrt(window * third_total)
    first_third = first_wide / math.sqrt(window * second_total)
    gram_first = jnp.dot(first_factor.T, first_factor, preferred_element_type=jnp.float32) / window

    gram_part = jnp.dot(third_factor.T, third_factor, preferred_element_type=jnp.float32)
    gram_part = ring_scatter(gram_part, "y")
    gram_part = ring_sum(gram_part, "zh")
    parts = ring_gather(gram_part, "y")
    inverse_second = inverse(parts, ring_places, gram_first, third_total)

    contracted = jnp.einsum("ijk,kr->ijr", tensor, third_factor, preferred_element_type=jnp.float32)
    partial_second = jnp.einsum(
        "ijr,ir->jr", contracted, first_second, precision=HIGHEST
    )
    row = scatter_sum(partial_second, NARROW)
    mttkrp_second = gather(row, NARROW)
    second_factor = jnp.dot(mttkrp_second, inverse_second, precision=HIGHEST).astype(jnp.bfloat16)

    gram_local = jnp.dot(second_factor.T, second_factor, preferred_element_type=jnp.float32)
    mine = scatter_sum(gram_local, WIDE)
    mine = join(mine, shift(mine, "core", 1), core)
    parts = quad_gather(mine, "zl")
    mine = ordered(parts, lax.axis_index("zl"))
    parts = quad_gather(mine, "x")
    inverse_third = inverse(parts, quad_places, gram_first, second_total)

    middle = jnp.einsum("ijk,jr->ikr", tensor, second_factor, preferred_element_type=jnp.float32)
    partial_third = jnp.einsum(
        "ikr,ir->kr", middle, first_third, precision=HIGHEST
    )
    mine, other = keep(partial_third, core)
    mine = mine + shift(other, "core", 1)
    mttkrp_third = scatter_sum(mine, CHIP)
    third_solution = jnp.dot(mttkrp_third, inverse_third, precision=HIGHEST)
    mine = gather(third_solution.astype(jnp.bfloat16), CHIP)
    third_new = join(mine, shift(mine, "core", 1), core)

    back = jnp.einsum("ijk,kr->ijr", tensor, third_new, preferred_element_type=jnp.float32)
    partial_first = jnp.einsum(
        "ijr,jr->ir", back, second_factor.astype(jnp.float32), precision=HIGHEST
    )
    partial_first = partial_first + shift(partial_first, "core", 1)
    scale = 1.0 / math.sqrt(second_total * third_total)
    partial_first = (ring_sum(partial_first, "x") * scale).astype(jnp.bfloat16)
    axes = ("zl",) + NARROW
    n = lax.axis_size(axes)
    copies = jnp.broadcast_to(partial_first[None], (n,) + partial_first.shape)
    first_mode = jnp.sum(exchange(copies, axes), axis=0, dtype=jnp.float32)
    return (second_factor, third_new, first_mode)


def solution(mesh):
    fine = Mesh(mesh.devices.reshape(4, 4, 2, 2, 4), WIDE + NARROW)
    in_specs = (P(None, WIDE, NARROW), P(), P(NARROW, None))
    out_specs = (P(WIDE, None), P(NARROW, None), P())
    return jax.shard_map(
        on_device, mesh=fine, in_specs=in_specs, out_specs=out_specs, check_vma=False
    )
```

```python
import functools
import math

import jax
import jax.numpy as jnp
from jax import lax
from jax.experimental import pallas as pl
from jax.experimental.pallas import tpu as pltpu
from jax.sharding import Mesh, PartitionSpec as P

ridge = 0.5
B = 16
WIDE = ("x", "zl", "core")
CHIP = ("x", "zl")
NARROW = ("zh", "y")
HIGHEST = lax.Precision.HIGHEST


def pieces(x):
    high = x.astype(jnp.bfloat16)
    rest = x - high.astype(jnp.float32)
    middle = rest.astype(jnp.bfloat16)
    low = (rest - middle.astype(jnp.float32)).astype(jnp.bfloat16)
    return high, middle, low


def split_pair(a, b):
    ah, am, al = pieces(a)
    bh, bm, bl = pieces(b)
    left = jnp.concatenate([ah, ah, am, ah, al, am], axis=0)
    return left, jnp.concatenate([bh, bm, bh, bl, bh, bm], axis=0)


def cross(a, b, **kw):
    return lax.dot_general(
        a, b, (((0,), (0,)), ((), ())), preferred_element_type=jnp.float32, **kw
    )


def inverse_kernel(places, total, *refs):
    part_refs, (f_ref, x_ref, m_ref, w_ref) = refs[:-4], refs[-4:]
    n = f_ref.shape[0]
    depth = part_refs[0].shape[0]
    for place, part_ref in zip(places(), part_refs):
        base = pl.multiple_of(place * depth, depth)
        here = (depth, n)
        diagonal = lax.broadcasted_iota(jnp.int32, here, 0) + base == lax.broadcasted_iota(jnp.int32, here, 1)
        m_ref[pl.ds(base, depth), :] = f_ref[pl.ds(base, depth), :] * (
            part_ref[...] * (1.0 / total)
        ) + jnp.where(diagonal, ridge, 0.0)
    row = lax.broadcasted_iota(jnp.int32, (B, n), 0)
    lane = lax.broadcasted_iota(jnp.int32, (B, n), 1)
    half_row = lax.broadcasted_iota(jnp.int32, (B, 128), 0)
    whole_row = lax.broadcasted_iota(jnp.int32, (n, n), 0)
    whole_lane = lax.broadcasted_iota(jnp.int32, (n, n), 1)

    def step(k, carry):
        panel, left, right = carry
        o = pl.multiple_of(k * B, B)
        cleared = (whole_row >= o) & (whole_lane >= o - B) & (whole_lane < o)
        m_ref[...] = jnp.where(cleared, 0.0, m_ref[...]) - cross(left, right)
        front = pltpu.roll(panel, n - o, 1)
        cols = [jnp.broadcast_to(front[:, j:j + 1], (B, 128)) for j in range(B)]
        inside = (lane >= o) & (lane < o + B)
        unit = jnp.where(lane - o == row, 1.0, 0.0)
        work = jnp.where(inside, unit, panel)
        parts = [work[:, t * 128:(t + 1) * 128] for t in range(n // 128)]
        for j in range(B):
            col = cols[j]
            scale = 1.0 / col[j:j + 1, :]
            other = half_row != j
            for t in range(len(parts)):
                pivot = parts[t][j:j + 1, :] * scale
                parts[t] = jnp.where(other, parts[t] - col * pivot, pivot)
            for m in range(j + 1, B):
                pivot = cols[m][j:j + 1, :] * scale
                cols[m] = jnp.where(other, cols[m] - col * pivot, pivot)
        solved = jnp.concatenate(parts, axis=1)
        left, right = split_pair(jnp.where(lane >= o + B, panel, 0.0), solved)
        ahead = split_pair(front[:, :128], front[:, :128])[0][:, B:2 * B]
        following = pl.multiple_of(jnp.minimum(o + B, n - B), B)
        panel_next = jnp.where(inside, 0.0, m_ref[pl.ds(following, B), :]) - cross(ahead, right)
        m_ref[pl.ds(o, B), :] = jnp.where(lane < o, panel, jnp.where(inside, unit, 0.0))
        w_ref[pl.ds(o, B), :] = jnp.where(lane < o + B, solved, 0.0)
        return panel_next, left, right

    nothing = jnp.zeros((6 * B, n), jnp.bfloat16)
    lax.fori_loop(0, n // B, step, (m_ref[0:B, :], nothing, nothing))
    x_ref[...] = cross(m_ref[...], w_ref[...], precision=HIGHEST)


def inverse(parts, places, gram_first, total):
    n = gram_first.shape[0]
    return pl.pallas_call(
        functools.partial(inverse_kernel, places, total),
        out_shape=jax.ShapeDtypeStruct((n, n), jnp.float32),
        in_specs=[pl.BlockSpec(memory_space=pltpu.VMEM)] * (len(parts) + 1),
        out_specs=pl.BlockSpec(memory_space=pltpu.VMEM),
        scratch_shapes=[pltpu.VMEM((n, n), jnp.float32), pltpu.VMEM((n, n), jnp.float32)],
        cost_estimate=pl.CostEstimate(flops=6 * 2 * n**3, bytes_accessed=8 * n * n, transcendentals=0),
        compiler_params=pltpu.CompilerParams(vmem_limit_bytes=8 << 20),
        name="inverse",
    )(*parts, gram_first)


def exchange(x, axes):
    return lax.all_to_all(x, axes, 0, 0, tiled=True)


def scatter_sum(x, axes):
    n = lax.axis_size(axes)
    return jnp.sum(exchange(x.reshape(n, x.shape[0] // n, x.shape[1]), axes), axis=0)


def gather(x, axes):
    n = lax.axis_size(axes)
    return exchange(jnp.broadcast_to(x[None], (n,) + x.shape), axes).reshape(n * x.shape[0], x.shape[1])


def shift(x, axis, d):
    n = lax.axis_size(axis)
    return lax.ppermute(x, axis, [(s, (s + d) % n) for s in range(n)])


def ring_scatter(x, axis):
    n = lax.axis_size(axis)
    me = lax.axis_index(axis)
    blocks = x.reshape(n, x.shape[0] // n, x.shape[1])
    take = lambda d: lax.dynamic_index_in_dim(blocks, lax.rem(me + d, n), 0, keepdims=False)
    arrived = [shift(take(d), axis, d) for d in range(1, n)]
    return sum(arrived, take(0))


def ring_sum(x, axis):
    return sum([shift(x, axis, d) for d in range(1, lax.axis_size(axis))], x)


def ring_gather(x, axis):
    return [x] + [shift(x, axis, d) for d in range(1, lax.axis_size(axis))]


def pair(x, axis, d):
    return lax.ppermute(x, axis, [(s, s ^ d) for s in range(lax.axis_size(axis))])


def quad_gather(x, axis):
    return [x] + [pair(x, axis, d) for d in (1, 2, 3)]


def ordered(parts, me):
    odd = lax.rem(me, 2) == 1
    low = [jnp.where(odd, parts[1], parts[0]), jnp.where(odd, parts[0], parts[1])]
    high = [jnp.where(odd, parts[3], parts[2]), jnp.where(odd, parts[2], parts[3])]
    up = me >= 2
    first = [jnp.where(up, h, l) for l, h in zip(low, high)]
    last = [jnp.where(up, l, h) for l, h in zip(low, high)]
    return jnp.concatenate(first + last, axis=0)


def keep(x, bit):
    half = x.shape[0] // 2
    low, high = x[:half], x[half:]
    return jnp.where(bit == 0, low, high), jnp.where(bit == 0, high, low)


def join(mine, theirs, bit):
    return jnp.where(
        bit == 0, jnp.concatenate([mine, theirs], 0), jnp.concatenate([theirs, mine], 0)
    )


def narrow_places():
    me = lax.axis_index("y")
    return [lax.rem(me + 4 - d, 4) for d in range(4)]


def wide_places():
    me = lax.axis_index("x")
    core = lax.axis_index("core")
    ring = [lax.rem(me + 4 - d, 4) for d in range(4)]
    return [core * 4 + r for r in ring] + [(1 - core) * 4 + r for r in ring]


def on_device(tensor, first_factor, third_factor):
    window, second_local, third_local = tensor.shape
    second_total = second_local * lax.axis_size(WIDE)
    third_total = third_local * lax.axis_size(NARROW)
    core = lax.axis_index("core")
    first_wide = first_factor.astype(jnp.float32)
    first_second = first_wide / math.sqrt(window * third_total)
    first_third = first_wide / math.sqrt(window * second_total)
    gram_first = jnp.dot(first_factor.T, first_factor, preferred_element_type=jnp.float32) / window

    gram_part = jnp.dot(third_factor.T, third_factor, preferred_element_type=jnp.float32)
    gram_part = ring_scatter(gram_part, "y")
    gram_part = ring_sum(gram_part, "zh")
    parts = ring_gather(gram_part, "y")
    inverse_second = inverse(parts, narrow_places, gram_first, third_total)

    contracted = jnp.einsum("ijk,kr->ijr", tensor, third_factor, preferred_element_type=jnp.float32)
    partial_second = jnp.einsum(
        "ijr,ir->jr", contracted, first_second, precision=HIGHEST
    )
    row = ring_scatter(partial_second, "y")
    row = ring_sum(row, "zh")
    parts = quad_gather(row, "y")
    mttkrp_second = jnp.concatenate(parts, axis=0)
    second_factor = jnp.dot(mttkrp_second, inverse_second, precision=HIGHEST).astype(jnp.bfloat16)
    second_factor = ordered(jnp.split(second_factor, 4, axis=0), lax.axis_index("y"))

    gram_local = jnp.dot(second_factor.T, second_factor, preferred_element_type=jnp.float32)
    mine, other = keep(gram_local, core)
    mine = mine + shift(other, "core", 1)
    mine = ring_scatter(mine, "x")
    mine = ring_sum(mine, "zl")
    parts = ring_gather(mine, "x")
    parts = parts + [shift(part, "core", 1) for part in parts]
    inverse_third = inverse(parts, wide_places, gram_first, second_total)

    middle = jnp.einsum("ijk,jr->ikr", tensor, second_factor, preferred_element_type=jnp.float32)
    partial_third = jnp.einsum(
        "ikr,ir->kr", middle, first_third, precision=HIGHEST
    )
    mine, other = keep(partial_third, core)
    mine = mine + shift(other, "core", 1)
    mttkrp_third = scatter_sum(mine, CHIP)
    third_solution = jnp.dot(mttkrp_third, inverse_third, precision=HIGHEST)
    mine = gather(third_solution.astype(jnp.bfloat16), CHIP)
    third_new = join(mine, shift(mine, "core", 1), core)

    back = jnp.einsum("ijk,kr->ijr", tensor, third_new, preferred_element_type=jnp.float32)
    partial_first = jnp.einsum(
        "ijr,jr->ir", back, second_factor.astype(jnp.float32), precision=HIGHEST
    )
    partial_first = partial_first + shift(partial_first, "core", 1)
    scale = 1.0 / math.sqrt(second_total * third_total)
    partial_first = (ring_sum(partial_first, "x") * scale).astype(jnp.bfloat16)
    axes = ("zl",) + NARROW
    n = lax.axis_size(axes)
    copies = jnp.broadcast_to(partial_first[None], (n,) + partial_first.shape)
    first_mode = jnp.sum(exchange(copies, axes), axis=0, dtype=jnp.float32)
    return (second_factor, third_new, first_mode)


def solution(mesh):
    fine = Mesh(mesh.devices.reshape(4, 4, 2, 2, 4), WIDE + NARROW)
    in_specs = (P(None, WIDE, NARROW), P(), P(NARROW, None))
    out_specs = (P(WIDE, None), P(NARROW, None), P())
    return jax.shard_map(
        on_device, mesh=fine, in_specs=in_specs, out_specs=out_specs, check_vma=False
    )
```

```python
import functools
import math

import jax
import jax.numpy as jnp
from jax import lax
from jax.experimental import pallas as pl
from jax.experimental.pallas import tpu as pltpu
from jax.sharding import Mesh, PartitionSpec as P

ridge = 0.5
B = 16
WIDE = ("x", "zl", "core")
CHIP = ("x", "zl")
NARROW = ("zh", "y")
HIGHEST = lax.Precision.HIGHEST


def pieces(x):
    high = x.astype(jnp.bfloat16)
    rest = x - high.astype(jnp.float32)
    middle = rest.astype(jnp.bfloat16)
    low = (rest - middle.astype(jnp.float32)).astype(jnp.bfloat16)
    return high, middle, low


def split_pair(a, b):
    ah, am, al = pieces(a)
    bh, bm, bl = pieces(b)
    left = jnp.concatenate([ah, ah, am, ah, al, am], axis=0)
    return left, jnp.concatenate([bh, bm, bh, bl, bh, bm], axis=0)


def cross(a, b, **kw):
    return lax.dot_general(
        a, b, (((0,), (0,)), ((), ())), preferred_element_type=jnp.float32, **kw
    )


def inverse_kernel(places, total, *refs):
    part_refs, (f_ref, x_ref, m_ref, w_ref) = refs[:-4], refs[-4:]
    n = f_ref.shape[0]
    depth = part_refs[0].shape[0]
    for place, part_ref in zip(places(), part_refs):
        base = pl.multiple_of(place * depth, depth)
        here = (depth, n)
        diagonal = lax.broadcasted_iota(jnp.int32, here, 0) + base == lax.broadcasted_iota(jnp.int32, here, 1)
        m_ref[pl.ds(base, depth), :] = f_ref[pl.ds(base, depth), :] * (
            part_ref[...] * (1.0 / total)
        ) + jnp.where(diagonal, ridge, 0.0)
    row = lax.broadcasted_iota(jnp.int32, (B, n), 0)
    lane = lax.broadcasted_iota(jnp.int32, (B, n), 1)
    half_row = lax.broadcasted_iota(jnp.int32, (B, 128), 0)
    whole_row = lax.broadcasted_iota(jnp.int32, (n, n), 0)
    whole_lane = lax.broadcasted_iota(jnp.int32, (n, n), 1)

    def step(k, carry):
        panel, left, right = carry
        o = pl.multiple_of(k * B, B)
        cleared = (whole_row >= o) & (whole_lane >= o - B) & (whole_lane < o)
        m_ref[...] = jnp.where(cleared, 0.0, m_ref[...]) - cross(left, right)
        front = pltpu.roll(panel, n - o, 1)
        cols = [jnp.broadcast_to(front[:, j:j + 1], (B, 128)) for j in range(B)]
        inside = (lane >= o) & (lane < o + B)
        unit = jnp.where(lane - o == row, 1.0, 0.0)
        work = jnp.where(inside, unit, panel)
        parts = [work[:, t * 128:(t + 1) * 128] for t in range(n // 128)]
        for j in range(B):
            col = cols[j]
            scale = 1.0 / col[j:j + 1, :]
            other = half_row != j
            for t in range(len(parts)):
                pivot = parts[t][j:j + 1, :] * scale
                parts[t] = jnp.where(other, parts[t] - col * pivot, pivot)
            for m in range(j + 1, B):
                pivot = cols[m][j:j + 1, :] * scale
                cols[m] = jnp.where(other, cols[m] - col * pivot, pivot)
        solved = jnp.concatenate(parts, axis=1)
        left, right = split_pair(jnp.where(lane >= o + B, panel, 0.0), solved)
        ahead = split_pair(front[:, :128], front[:, :128])[0][:, B:2 * B]
        following = pl.multiple_of(jnp.minimum(o + B, n - B), B)
        panel_next = jnp.where(inside, 0.0, m_ref[pl.ds(following, B), :]) - cross(ahead, right)
        m_ref[pl.ds(o, B), :] = jnp.where(lane < o, panel, jnp.where(inside, unit, 0.0))
        w_ref[pl.ds(o, B), :] = jnp.where(lane < o + B, solved, 0.0)
        return panel_next, left, right

    nothing = jnp.zeros((6 * B, n), jnp.bfloat16)
    lax.fori_loop(0, n // B, step, (m_ref[0:B, :], nothing, nothing))
    x_ref[...] = cross(m_ref[...], w_ref[...], precision=HIGHEST)


def inverse(parts, places, gram_first, total):
    n = gram_first.shape[0]
    return pl.pallas_call(
        functools.partial(inverse_kernel, places, total),
        out_shape=jax.ShapeDtypeStruct((n, n), jnp.float32),
        in_specs=[pl.BlockSpec(memory_space=pltpu.VMEM)] * (len(parts) + 1),
        out_specs=pl.BlockSpec(memory_space=pltpu.VMEM),
        scratch_shapes=[pltpu.VMEM((n, n), jnp.float32), pltpu.VMEM((n, n), jnp.float32)],
        cost_estimate=pl.CostEstimate(flops=6 * 2 * n**3, bytes_accessed=8 * n * n, transcendentals=0),
        compiler_params=pltpu.CompilerParams(vmem_limit_bytes=8 << 20),
        name="inverse",
    )(*parts, gram_first)


def exchange(x, axes):
    return lax.all_to_all(x, axes, 0, 0, tiled=True)


def scatter_sum(x, axes):
    n = lax.axis_size(axes)
    return jnp.sum(exchange(x.reshape(n, x.shape[0] // n, x.shape[1]), axes), axis=0)


def gather(x, axes):
    n = lax.axis_size(axes)
    return exchange(jnp.broadcast_to(x[None], (n,) + x.shape), axes).reshape(n * x.shape[0], x.shape[1])


def shift(x, axis, d):
    n = lax.axis_size(axis)
    return lax.ppermute(x, axis, [(s, (s + d) % n) for s in range(n)])


def ring_scatter(x, axis):
    n = lax.axis_size(axis)
    me = lax.axis_index(axis)
    blocks = x.reshape(n, x.shape[0] // n, x.shape[1])
    take = lambda d: lax.dynamic_index_in_dim(blocks, lax.rem(me + d, n), 0, keepdims=False)
    arrived = [shift(take(d), axis, d) for d in range(1, n)]
    return sum(arrived, take(0))


def ring_sum(x, axis):
    return sum([shift(x, axis, d) for d in range(1, lax.axis_size(axis))], x)


def ring_gather(x, axis):
    return [x] + [shift(x, axis, d) for d in range(1, lax.axis_size(axis))]


def pair(x, axis, d):
    return lax.ppermute(x, axis, [(s, s ^ d) for s in range(lax.axis_size(axis))])


def quad_gather(x, axis):
    return [x] + [pair(x, axis, d) for d in (1, 2, 3)]


def ordered(parts, me):
    odd = lax.rem(me, 2) == 1
    low = [jnp.where(odd, parts[1], parts[0]), jnp.where(odd, parts[0], parts[1])]
    high = [jnp.where(odd, parts[3], parts[2]), jnp.where(odd, parts[2], parts[3])]
    up = me >= 2
    first = [jnp.where(up, h, l) for l, h in zip(low, high)]
    last = [jnp.where(up, l, h) for l, h in zip(low, high)]
    return jnp.concatenate(first + last, axis=0)


def keep(x, bit):
    half = x.shape[0] // 2
    low, high = x[:half], x[half:]
    return jnp.where(bit == 0, low, high), jnp.where(bit == 0, high, low)


def join(mine, theirs, bit):
    return jnp.where(
        bit == 0, jnp.concatenate([mine, theirs], 0), jnp.concatenate([theirs, mine], 0)
    )


def narrow_places():
    me = lax.axis_index("y")
    return [lax.rem(me + 4 - d, 4) for d in range(4)]


def wide_places():
    me = lax.axis_index("x")
    core = lax.axis_index("core")
    ring = [lax.rem(me + 4 - d, 4) for d in range(4)]
    return [core * 4 + r for r in ring] + [(1 - core) * 4 + r for r in ring]


def on_device(tensor, first_factor, third_factor):
    window, second_local, third_local = tensor.shape
    second_total = second_local * lax.axis_size(WIDE)
    third_total = third_local * lax.axis_size(NARROW)
    core = lax.axis_index("core")
    first_wide = first_factor.astype(jnp.float32)
    first_second = first_wide / math.sqrt(window * third_total)
    first_third = first_wide / math.sqrt(window * second_total)
    gram_first = jnp.dot(first_factor.T, first_factor, preferred_element_type=jnp.float32) / window

    gram_part = jnp.dot(third_factor.T, third_factor, preferred_element_type=jnp.float32)
    gram_part = ring_scatter(gram_part, "y")
    gram_part = ring_sum(gram_part, "zh")
    parts = ring_gather(gram_part, "y")
    inverse_second = inverse(parts, narrow_places, gram_first, third_total)

    contracted = jnp.einsum("ijk,kr->ijr", tensor, third_factor, preferred_element_type=jnp.float32)
    partial_second = jnp.einsum(
        "ijr,ir->jr", contracted, first_second, precision=HIGHEST
    )
    row = ring_scatter(partial_second, "y")
    row = ring_sum(row, "zh")
    row = jnp.dot(row, inverse_second, precision=HIGHEST).astype(jnp.bfloat16)
    second_factor = ordered(quad_gather(row, "y"), lax.axis_index("y"))

    gram_local = jnp.dot(second_factor.T, second_factor, preferred_element_type=jnp.float32)
    mine, other = keep(gram_local, core)
    mine = mine + shift(other, "core", 1)
    mine = ring_scatter(mine, "x")
    mine = ring_sum(mine, "zl")
    parts = ring_gather(mine, "x")
    parts = parts + [shift(part, "core", 1) for part in parts]
    inverse_third = inverse(parts, wide_places, gram_first, second_total)

    middle = jnp.einsum("ijk,jr->ikr", tensor, second_factor, preferred_element_type=jnp.float32)
    partial_third = jnp.einsum(
        "ikr,ir->kr", middle, first_third, precision=HIGHEST
    )
    mine, other = keep(partial_third, core)
    mine = mine + shift(other, "core", 1)
    mttkrp_third = scatter_sum(mine, CHIP)
    third_solution = jnp.dot(mttkrp_third, inverse_third, precision=HIGHEST)
    mine = gather(third_solution.astype(jnp.bfloat16), CHIP)
    third_new = join(mine, shift(mine, "core", 1), core)

    back = jnp.einsum("ijk,kr->ijr", tensor, third_new, preferred_element_type=jnp.float32)
    partial_first = jnp.einsum(
        "ijr,jr->ir", back, second_factor.astype(jnp.float32), precision=HIGHEST
    )
    partial_first = partial_first + shift(partial_first, "core", 1)
    scale = 1.0 / math.sqrt(second_total * third_total)
    partial_first = (ring_sum(partial_first, "x") * scale).astype(jnp.bfloat16)
    axes = ("zl",) + NARROW
    n = lax.axis_size(axes)
    copies = jnp.broadcast_to(partial_first[None], (n,) + partial_first.shape)
    first_mode = jnp.sum(exchange(copies, axes), axis=0, dtype=jnp.float32)
    return (second_factor, third_new, first_mode)


def solution(mesh):
    fine = Mesh(mesh.devices.reshape(4, 4, 2, 2, 4), WIDE + NARROW)
    in_specs = (P(None, WIDE, NARROW), P(), P(NARROW, None))
    out_specs = (P(WIDE, None), P(NARROW, None), P())
    return jax.shard_map(
        on_device, mesh=fine, in_specs=in_specs, out_specs=out_specs, check_vma=False
    )
```

```python
import functools
import math

import jax
import jax.numpy as jnp
from jax import lax
from jax.experimental import pallas as pl
from jax.experimental.pallas import tpu as pltpu
from jax.sharding import Mesh, PartitionSpec as P

ridge = 0.5
B = 16
WIDE = ("x", "zl", "core")
CHIP = ("x", "zl")
NARROW = ("zh", "y")
HIGHEST = lax.Precision.HIGHEST


def pieces(x):
    high = x.astype(jnp.bfloat16)
    rest = x - high.astype(jnp.float32)
    middle = rest.astype(jnp.bfloat16)
    low = (rest - middle.astype(jnp.float32)).astype(jnp.bfloat16)
    return high, middle, low


def split_pair(a, b):
    ah, am, al = pieces(a)
    bh, bm, bl = pieces(b)
    left = jnp.concatenate([ah, ah, am, ah, al, am], axis=0)
    return left, jnp.concatenate([bh, bm, bh, bl, bh, bm], axis=0)


def cross(a, b, **kw):
    return lax.dot_general(
        a, b, (((0,), (0,)), ((), ())), preferred_element_type=jnp.float32, **kw
    )


def inverse_kernel(places, total, *refs):
    part_refs, (f_ref, x_ref, m_ref, w_ref) = refs[:-4], refs[-4:]
    n = f_ref.shape[0]
    depth = part_refs[0].shape[0]
    for place, part_ref in zip(places(), part_refs):
        base = pl.multiple_of(place * depth, depth)
        here = (depth, n)
        diagonal = lax.broadcasted_iota(jnp.int32, here, 0) + base == lax.broadcasted_iota(jnp.int32, here, 1)
        m_ref[pl.ds(base, depth), :] = f_ref[pl.ds(base, depth), :] * (
            part_ref[...] * (1.0 / total)
        ) + jnp.where(diagonal, ridge, 0.0)
    row = lax.broadcasted_iota(jnp.int32, (B, n), 0)
    lane = lax.broadcasted_iota(jnp.int32, (B, n), 1)
    half_row = lax.broadcasted_iota(jnp.int32, (B, 128), 0)
    whole_row = lax.broadcasted_iota(jnp.int32, (n, n), 0)
    whole_lane = lax.broadcasted_iota(jnp.int32, (n, n), 1)

    def step(k, carry):
        panel, left, right = carry
        o = pl.multiple_of(k * B, B)
        cleared = (whole_row >= o) & (whole_lane >= o - B) & (whole_lane < o)
        m_ref[...] = jnp.where(cleared, 0.0, m_ref[...]) - cross(left, right)
        front = pltpu.roll(panel, n - o, 1)
        cols = [jnp.broadcast_to(front[:, j:j + 1], (B, 128)) for j in range(B)]
        inside = (lane >= o) & (lane < o + B)
        unit = jnp.where(lane - o == row, 1.0, 0.0)
        work = jnp.where(inside, unit, panel)
        parts = [work[:, t * 128:(t + 1) * 128] for t in range(n // 128)]
        for j in range(B):
            col = cols[j]
            scale = 1.0 / col[j:j + 1, :]
            other = half_row != j
            for t in range(len(parts)):
                pivot = parts[t][j:j + 1, :] * scale
                parts[t] = jnp.where(other, parts[t] - col * pivot, pivot)
            for m in range(j + 1, B):
                pivot = cols[m][j:j + 1, :] * scale
                cols[m] = jnp.where(other, cols[m] - col * pivot, pivot)
        solved = jnp.concatenate(parts, axis=1)
        left, right = split_pair(jnp.where(lane >= o + B, panel, 0.0), solved)
        ahead = split_pair(front[:, :128], front[:, :128])[0][:, B:2 * B]
        following = pl.multiple_of(jnp.minimum(o + B, n - B), B)
        panel_next = jnp.where(inside, 0.0, m_ref[pl.ds(following, B), :]) - cross(ahead, right)
        m_ref[pl.ds(o, B), :] = jnp.where(lane < o, panel, jnp.where(inside, unit, 0.0))
        w_ref[pl.ds(o, B), :] = jnp.where(lane < o + B, solved, 0.0)
        return panel_next, left, right

    nothing = jnp.zeros((6 * B, n), jnp.bfloat16)
    lax.fori_loop(0, n // B, step, (m_ref[0:B, :], nothing, nothing))
    x_ref[...] = cross(m_ref[...], w_ref[...], precision=HIGHEST)


def inverse(parts, places, gram_first, total):
    n = gram_first.shape[0]
    return pl.pallas_call(
        functools.partial(inverse_kernel, places, total),
        out_shape=jax.ShapeDtypeStruct((n, n), jnp.float32),
        in_specs=[pl.BlockSpec(memory_space=pltpu.VMEM)] * (len(parts) + 1),
        out_specs=pl.BlockSpec(memory_space=pltpu.VMEM),
        scratch_shapes=[pltpu.VMEM((n, n), jnp.float32), pltpu.VMEM((n, n), jnp.float32)],
        cost_estimate=pl.CostEstimate(flops=6 * 2 * n**3, bytes_accessed=8 * n * n, transcendentals=0),
        compiler_params=pltpu.CompilerParams(vmem_limit_bytes=8 << 20),
        name="inverse",
    )(*parts, gram_first)


def exchange(x, axes):
    return lax.all_to_all(x, axes, 0, 0, tiled=True)


def scatter_sum(x, axes):
    n = lax.axis_size(axes)
    return jnp.sum(exchange(x.reshape(n, x.shape[0] // n, x.shape[1]), axes), axis=0)


def gather(x, axes):
    n = lax.axis_size(axes)
    return exchange(jnp.broadcast_to(x[None], (n,) + x.shape), axes).reshape(n * x.shape[0], x.shape[1])


def pair(x, axis, d):
    return lax.ppermute(x, axis, [(i, i ^ d) for i in range(lax.axis_size(axis))])


def keep(x, bit):
    half = x.shape[0] // 2
    low, high = x[:half], x[half:]
    return jnp.where(bit == 0, low, high), jnp.where(bit == 0, high, low)


def join(mine, theirs, bit):
    return jnp.where(
        bit == 0, jnp.concatenate([mine, theirs], 0), jnp.concatenate([theirs, mine], 0)
    )


def quarter_bits(axis):
    me = lax.axis_index(axis)
    high = me // 2
    low = lax.rem(me, 2)
    return lax.rem(low + high, 2), high


def halve(x, axis, d, bit):
    mine, other = keep(x, bit)
    return mine + pair(other, axis, d)


def grow(x, axis, d, bit):
    return join(x, pair(x, axis, d), bit)


def whole():
    return [0]


def on_device(tensor, first_factor, third_factor):
    window, second_local, third_local = tensor.shape
    second_total = second_local * lax.axis_size(WIDE)
    third_total = third_local * lax.axis_size(NARROW)
    core = lax.axis_index("core")
    first_wide = first_factor.astype(jnp.float32)
    first_second = first_wide / math.sqrt(window * third_total)
    first_third = first_wide / math.sqrt(window * second_total)
    gram_first = jnp.dot(first_factor.T, first_factor, preferred_element_type=jnp.float32) / window

    gram_part = jnp.dot(third_factor.T, third_factor, preferred_element_type=jnp.float32)
    near, far = quarter_bits("y")
    gram_part = halve(gram_part, "y", 1, near)
    gram_part = halve(gram_part, "y", 3, far)
    gram_part = gram_part + pair(gram_part, "zh", 1)
    gram_part = grow(gram_part, "y", 3, far)
    gram_third = grow(gram_part, "y", 1, near)
    inverse_second = inverse([gram_third], whole, gram_first, third_total)

    contracted = jnp.einsum("ijk,kr->ijr", tensor, third_factor, preferred_element_type=jnp.float32)
    partial_second = jnp.sum(contracted * first_second[:, None, :], axis=0)
    row = halve(partial_second, "y", 1, near)
    row = halve(row, "y", 3, far)
    row = row + pair(row, "zh", 1)
    row = jnp.dot(row, inverse_second, precision=HIGHEST).astype(jnp.bfloat16)
    row = grow(row, "y", 3, far)
    second_factor = grow(row, "y", 1, near)

    first_third, tensor = lax.optimization_barrier((first_third, tensor))
    gram_local = jnp.dot(second_factor.T, second_factor, preferred_element_type=jnp.float32)
    near, far = quarter_bits("x")
    mine = halve(gram_local, "core", 1, core)
    mine = halve(mine, "x", 1, near)
    mine = halve(mine, "x", 3, far)
    mine = mine + pair(mine, "zl", 1)
    mine = mine + pair(mine, "zl", 2)
    mine = grow(mine, "x", 3, far)
    mine = grow(mine, "x", 1, near)
    gram_second = grow(mine, "core", 1, core)
    inverse_third = inverse([gram_second], whole, gram_first, second_total)

    middle = jnp.einsum("ijk,jr->ikr", tensor, second_factor, preferred_element_type=jnp.float32)
    partial_third = jnp.sum(middle * first_third[:, None, :], axis=0)
    mine = halve(partial_third, "core", 1, core)
    mttkrp_third = scatter_sum(mine, CHIP)
    third_solution = jnp.dot(mttkrp_third, inverse_third, precision=HIGHEST)
    mine = gather(third_solution.astype(jnp.bfloat16), CHIP)
    third_new = grow(mine, "core", 1, core)

    back = jnp.einsum("ijk,kr->ijr", tensor, third_new, preferred_element_type=jnp.float32)
    partial_first = jnp.sum(back * second_factor.astype(jnp.float32)[None], axis=1)
    partial_first = partial_first + pair(partial_first, "core", 1)
    partial_first = partial_first + pair(partial_first, "x", 1)
    partial_first = partial_first + pair(partial_first, "x", 3)
    scale = 1.0 / math.sqrt(second_total * third_total)
    partial_first = (partial_first * scale).astype(jnp.bfloat16)
    axes = ("zl",) + NARROW
    n = lax.axis_size(axes)
    copies = jnp.broadcast_to(partial_first[None], (n,) + partial_first.shape)
    first_mode = jnp.sum(exchange(copies, axes), axis=0, dtype=jnp.float32)
    return (second_factor, third_new, first_mode)


def solution(mesh):
    fine = Mesh(mesh.devices.reshape(4, 4, 2, 2, 4), WIDE + NARROW)
    in_specs = (P(None, WIDE, NARROW), P(), P(NARROW, None))
    out_specs = (P(WIDE, None), P(NARROW, None), P())
    return jax.shard_map(
        on_device, mesh=fine, in_specs=in_specs, out_specs=out_specs, check_vma=False
    )
```

```python
import functools
import math

import jax
import jax.numpy as jnp
from jax import lax
from jax.experimental import pallas as pl
from jax.experimental.pallas import tpu as pltpu
from jax.sharding import Mesh, PartitionSpec as P

ridge = 0.5
B = 16
WIDE = ("x", "zl", "core")
CHIP = ("x", "zl")
NARROW = ("zh", "y")
HIGHEST = lax.Precision.HIGHEST


def pieces(x):
    high = x.astype(jnp.bfloat16)
    rest = x - high.astype(jnp.float32)
    middle = rest.astype(jnp.bfloat16)
    low = (rest - middle.astype(jnp.float32)).astype(jnp.bfloat16)
    return high, middle, low


def split_pair(a, b):
    ah, am, al = pieces(a)
    bh, bm, bl = pieces(b)
    left = jnp.concatenate([ah, ah, am, ah, al, am], axis=0)
    return left, jnp.concatenate([bh, bm, bh, bl, bh, bm], axis=0)


def cross(a, b, **kw):
    return lax.dot_general(
        a, b, (((0,), (0,)), ((), ())), preferred_element_type=jnp.float32, **kw
    )


def inverse_kernel(places, total, *refs):
    part_refs, (f_ref, x_ref, m_ref, w_ref) = refs[:-4], refs[-4:]
    n = f_ref.shape[0]
    blocks = [(ref, t, len(group), place) for ref, group in zip(part_refs, places()) for t, place in enumerate(group)]
    for part_ref, t, count, place in blocks:
        depth = part_ref.shape[0] // count
        base = pl.multiple_of(place * depth, depth)
        here = (depth, n)
        diagonal = lax.broadcasted_iota(jnp.int32, here, 0) + base == lax.broadcasted_iota(jnp.int32, here, 1)
        m_ref[pl.ds(base, depth), :] = f_ref[pl.ds(base, depth), :] * (
            part_ref[t * depth:(t + 1) * depth, :] * (1.0 / total)
        ) + jnp.where(diagonal, ridge, 0.0)
    row = lax.broadcasted_iota(jnp.int32, (B, n), 0)
    lane = lax.broadcasted_iota(jnp.int32, (B, n), 1)
    half_row = lax.broadcasted_iota(jnp.int32, (B, 128), 0)
    whole_row = lax.broadcasted_iota(jnp.int32, (n, n), 0)
    whole_lane = lax.broadcasted_iota(jnp.int32, (n, n), 1)

    def step(k, carry):
        panel, left, right = carry
        o = pl.multiple_of(k * B, B)
        cleared = (whole_row >= o) & (whole_lane >= o - B) & (whole_lane < o)
        m_ref[...] = jnp.where(cleared, 0.0, m_ref[...]) - cross(left, right)
        front = pltpu.roll(panel, n - o, 1)
        cols = [jnp.broadcast_to(front[:, j:j + 1], (B, 128)) for j in range(B)]
        inside = (lane >= o) & (lane < o + B)
        unit = jnp.where(lane - o == row, 1.0, 0.0)
        work = jnp.where(inside, unit, panel)
        parts = [work[:, t * 128:(t + 1) * 128] for t in range(n // 128)]
        for j in range(B):
            col = cols[j]
            scale = 1.0 / col[j:j + 1, :]
            other = half_row != j
            for t in range(len(parts)):
                pivot = parts[t][j:j + 1, :] * scale
                parts[t] = jnp.where(other, parts[t] - col * pivot, pivot)
            for m in range(j + 1, B):
                pivot = cols[m][j:j + 1, :] * scale
                cols[m] = jnp.where(other, cols[m] - col * pivot, pivot)
        solved = jnp.concatenate(parts, axis=1)
        left, right = split_pair(jnp.where(lane >= o + B, panel, 0.0), solved)
        ahead = split_pair(front[:, :128], front[:, :128])[0][:, B:2 * B]
        following = pl.multiple_of(jnp.minimum(o + B, n - B), B)
        panel_next = jnp.where(inside, 0.0, m_ref[pl.ds(following, B), :]) - cross(ahead, right)
        m_ref[pl.ds(o, B), :] = jnp.where(lane < o, panel, jnp.where(inside, unit, 0.0))
        w_ref[pl.ds(o, B), :] = jnp.where(lane < o + B, solved, 0.0)
        return panel_next, left, right

    nothing = jnp.zeros((6 * B, n), jnp.bfloat16)
    lax.fori_loop(0, n // B, step, (m_ref[0:B, :], nothing, nothing))
    x_ref[...] = cross(m_ref[...], w_ref[...], precision=HIGHEST)


def inverse(parts, places, gram_first, total):
    n = gram_first.shape[0]
    return pl.pallas_call(
        functools.partial(inverse_kernel, places, total),
        out_shape=jax.ShapeDtypeStruct((n, n), jnp.float32),
        in_specs=[pl.BlockSpec(memory_space=pltpu.VMEM)] * (len(parts) + 1),
        out_specs=pl.BlockSpec(memory_space=pltpu.VMEM),
        scratch_shapes=[pltpu.VMEM((n, n), jnp.float32), pltpu.VMEM((n, n), jnp.float32)],
        cost_estimate=pl.CostEstimate(flops=6 * 2 * n**3, bytes_accessed=8 * n * n, transcendentals=0),
        compiler_params=pltpu.CompilerParams(vmem_limit_bytes=8 << 20),
        name="inverse",
    )(*parts, gram_first)


def exchange(x, axes):
    return lax.all_to_all(x, axes, 0, 0, tiled=True)


def scatter_sum(x, axes):
    n = lax.axis_size(axes)
    return jnp.sum(exchange(x.reshape(n, x.shape[0] // n, x.shape[1]), axes), axis=0)


def gather(x, axes):
    n = lax.axis_size(axes)
    return exchange(jnp.broadcast_to(x[None], (n,) + x.shape), axes).reshape(n * x.shape[0], x.shape[1])


def shift(x, axis, d):
    n = lax.axis_size(axis)
    return lax.ppermute(x, axis, [(s, (s + d) % n) for s in range(n)])


def ring_scatter(x, axis):
    n = lax.axis_size(axis)
    me = lax.axis_index(axis)
    blocks = x.reshape(n, x.shape[0] // n, x.shape[1])
    take = lambda d: lax.dynamic_index_in_dim(blocks, lax.rem(me + d, n), 0, keepdims=False)
    arrived = [shift(take(d), axis, d) for d in range(1, n)]
    return sum(arrived, take(0))


def ring_sum(x, axis):
    return sum([shift(x, axis, d) for d in range(1, lax.axis_size(axis))], x)


def ring_gather(x, axis):
    return [x] + [shift(x, axis, d) for d in range(1, lax.axis_size(axis))]


def pair(x, axis, d):
    return lax.ppermute(x, axis, [(s, s ^ d) for s in range(lax.axis_size(axis))])


def quad_gather(x, axis):
    return [x] + [pair(x, axis, d) for d in (1, 2, 3)]


def ordered(parts, me):
    odd = lax.rem(me, 2) == 1
    low = [jnp.where(odd, parts[1], parts[0]), jnp.where(odd, parts[0], parts[1])]
    high = [jnp.where(odd, parts[3], parts[2]), jnp.where(odd, parts[2], parts[3])]
    up = me >= 2
    first = [jnp.where(up, h, l) for l, h in zip(low, high)]
    last = [jnp.where(up, l, h) for l, h in zip(low, high)]
    return jnp.concatenate(first + last, axis=0)


def keep(x, bit):
    half = x.shape[0] // 2
    low, high = x[:half], x[half:]
    return jnp.where(bit == 0, low, high), jnp.where(bit == 0, high, low)


def join(mine, theirs, bit):
    return jnp.where(
        bit == 0, jnp.concatenate([mine, theirs], 0), jnp.concatenate([theirs, mine], 0)
    )


def narrow_places():
    me = lax.axis_index("y")
    return [(lax.rem(me + 4 - d, 4),) for d in range(4)]


def wide_places():
    me = lax.axis_index("x")
    ring = [lax.rem(me + 4 - d, 4) for d in range(4)]
    return [(r, r + 4) for r in ring]


def on_device(tensor, first_factor, third_factor):
    window, second_local, third_local = tensor.shape
    second_total = second_local * lax.axis_size(WIDE)
    third_total = third_local * lax.axis_size(NARROW)
    core = lax.axis_index("core")
    first_wide = first_factor.astype(jnp.float32)
    first_second = first_wide / math.sqrt(window * third_total)
    first_third = first_wide / math.sqrt(window * second_total)
    gram_first = jnp.dot(first_factor.T, first_factor, preferred_element_type=jnp.float32) / window

    gram_part = jnp.dot(third_factor.T, third_factor, preferred_element_type=jnp.float32)
    gram_part = ring_scatter(gram_part, "y")
    gram_part = ring_sum(gram_part, "zh")
    parts = ring_gather(gram_part, "y")
    inverse_second = inverse(parts, narrow_places, gram_first, third_total)

    contracted = jnp.einsum("ijk,kr->ijr", tensor, third_factor, preferred_element_type=jnp.float32)
    partial_second = jnp.sum(contracted * first_second[:, None, :], axis=0)
    row = ring_scatter(partial_second, "y")
    row = ring_sum(row, "zh")
    row = jnp.dot(row, inverse_second, precision=HIGHEST).astype(jnp.bfloat16)
    second_factor = ordered(quad_gather(row, "y"), lax.axis_index("y"))

    first_third, tensor = lax.optimization_barrier((first_third, tensor))
    gram_local = jnp.dot(second_factor.T, second_factor, preferred_element_type=jnp.float32)
    mine, other = keep(gram_local, core)
    mine = mine + shift(other, "core", 1)
    mine = ring_scatter(mine, "x")
    mine = ring_sum(mine, "zl")
    mine = join(mine, shift(mine, "core", 1), core)
    parts = ring_gather(mine, "x")
    inverse_third = inverse(parts, wide_places, gram_first, second_total)

    middle = jnp.einsum("ijk,jr->ikr", tensor, second_factor, preferred_element_type=jnp.float32)
    partial_third = jnp.sum(middle * first_third[:, None, :], axis=0)
    mine, other = keep(partial_third, core)
    mine = mine + shift(other, "core", 1)
    mttkrp_third = scatter_sum(mine, CHIP)
    third_solution = jnp.dot(mttkrp_third, inverse_third, precision=HIGHEST)
    mine = gather(third_solution.astype(jnp.bfloat16), CHIP)
    third_new = join(mine, shift(mine, "core", 1), core)

    back = jnp.einsum("ijk,kr->ijr", tensor, third_new, preferred_element_type=jnp.float32)
    partial_first = jnp.sum(back * second_factor.astype(jnp.float32)[None], axis=1)
    partial_first = partial_first + shift(partial_first, "core", 1)
    scale = 1.0 / math.sqrt(second_total * third_total)
    partial_first = (ring_sum(partial_first, "x") * scale).astype(jnp.bfloat16)
    axes = ("zl",) + NARROW
    n = lax.axis_size(axes)
    copies = jnp.broadcast_to(partial_first[None], (n,) + partial_first.shape)
    first_mode = jnp.sum(exchange(copies, axes), axis=0, dtype=jnp.float32)
    return (second_factor, third_new, first_mode)


def solution(mesh):
    fine = Mesh(mesh.devices.reshape(4, 4, 2, 2, 4), WIDE + NARROW)
    in_specs = (P(None, WIDE, NARROW), P(), P(NARROW, None))
    out_specs = (P(WIDE, None), P(NARROW, None), P())
    return jax.shard_map(
        on_device, mesh=fine, in_specs=in_specs, out_specs=out_specs, check_vma=False
    )
```

```python
import functools
import math

import jax
import jax.numpy as jnp
from jax import lax
from jax.experimental import pallas as pl
from jax.experimental.pallas import tpu as pltpu
from jax.sharding import Mesh, PartitionSpec as P

ridge = 0.5
B = 16
WIDE = ("x", "zl", "core")
CHIP = ("x", "zl")
NARROW = ("zh", "y")
HIGHEST = lax.Precision.HIGHEST


def pieces(x):
    high = x.astype(jnp.bfloat16)
    rest = x - high.astype(jnp.float32)
    middle = rest.astype(jnp.bfloat16)
    low = (rest - middle.astype(jnp.float32)).astype(jnp.bfloat16)
    return high, middle, low


def split_pair(a, b):
    ah, am, al = pieces(a)
    bh, bm, bl = pieces(b)
    left = jnp.concatenate([ah, ah, am, ah, al, am], axis=0)
    return left, jnp.concatenate([bh, bm, bh, bl, bh, bm], axis=0)


def cross(a, b, **kw):
    return lax.dot_general(
        a, b, (((0,), (0,)), ((), ())), preferred_element_type=jnp.float32, **kw
    )


def inverse_kernel(places, total, *refs):
    part_refs, (f_ref, x_ref, m_ref, w_ref) = refs[:-4], refs[-4:]
    n = f_ref.shape[0]
    blocks = [(ref, t, len(group), place) for ref, group in zip(part_refs, places()) for t, place in enumerate(group)]
    for part_ref, t, count, place in blocks:
        depth = part_ref.shape[0] // count
        base = pl.multiple_of(place * depth, depth)
        here = (depth, n)
        diagonal = lax.broadcasted_iota(jnp.int32, here, 0) + base == lax.broadcasted_iota(jnp.int32, here, 1)
        m_ref[pl.ds(base, depth), :] = f_ref[pl.ds(base, depth), :] * (
            part_ref[t * depth:(t + 1) * depth, :] * (1.0 / total)
        ) + jnp.where(diagonal, ridge, 0.0)
    row = lax.broadcasted_iota(jnp.int32, (B, n), 0)
    lane = lax.broadcasted_iota(jnp.int32, (B, n), 1)
    half_row = lax.broadcasted_iota(jnp.int32, (B, 128), 0)
    whole_row = lax.broadcasted_iota(jnp.int32, (n, n), 0)
    whole_lane = lax.broadcasted_iota(jnp.int32, (n, n), 1)

    def step(k, carry):
        panel, left, right = carry
        o = pl.multiple_of(k * B, B)
        cleared = (whole_row >= o) & (whole_lane >= o - B) & (whole_lane < o)
        m_ref[...] = jnp.where(cleared, 0.0, m_ref[...]) - cross(left, right)
        front = pltpu.roll(panel, n - o, 1)
        cols = [jnp.broadcast_to(front[:, j:j + 1], (B, 128)) for j in range(B)]
        inside = (lane >= o) & (lane < o + B)
        unit = jnp.where(lane - o == row, 1.0, 0.0)
        work = jnp.where(inside, unit, panel)
        parts = [work[:, t * 128:(t + 1) * 128] for t in range(n // 128)]
        for j in range(B):
            col = cols[j]
            scale = 1.0 / col[j:j + 1, :]
            other = half_row != j
            for t in range(len(parts)):
                pivot = parts[t][j:j + 1, :] * scale
                parts[t] = jnp.where(other, parts[t] - col * pivot, pivot)
            for m in range(j + 1, B):
                pivot = cols[m][j:j + 1, :] * scale
                cols[m] = jnp.where(other, cols[m] - col * pivot, pivot)
        solved = jnp.concatenate(parts, axis=1)
        left, right = split_pair(jnp.where(lane >= o + B, panel, 0.0), solved)
        ahead = split_pair(front[:, :128], front[:, :128])[0][:, B:2 * B]
        following = pl.multiple_of(jnp.minimum(o + B, n - B), B)
        panel_next = jnp.where(inside, 0.0, m_ref[pl.ds(following, B), :]) - cross(ahead, right)
        m_ref[pl.ds(o, B), :] = jnp.where(lane < o, panel, jnp.where(inside, unit, 0.0))
        w_ref[pl.ds(o, B), :] = jnp.where(lane < o + B, solved, 0.0)
        return panel_next, left, right

    nothing = jnp.zeros((6 * B, n), jnp.bfloat16)
    lax.fori_loop(0, n // B, step, (m_ref[0:B, :], nothing, nothing))
    x_ref[...] = cross(m_ref[...], w_ref[...], precision=HIGHEST)


def inverse(parts, places, gram_first, total):
    n = gram_first.shape[0]
    return pl.pallas_call(
        functools.partial(inverse_kernel, places, total),
        out_shape=jax.ShapeDtypeStruct((n, n), jnp.float32),
        in_specs=[pl.BlockSpec(memory_space=pltpu.VMEM)] * (len(parts) + 1),
        out_specs=pl.BlockSpec(memory_space=pltpu.VMEM),
        scratch_shapes=[pltpu.VMEM((n, n), jnp.float32), pltpu.VMEM((n, n), jnp.float32)],
        cost_estimate=pl.CostEstimate(flops=6 * 2 * n**3, bytes_accessed=8 * n * n, transcendentals=0),
        compiler_params=pltpu.CompilerParams(vmem_limit_bytes=8 << 20),
        name="inverse",
    )(*parts, gram_first)


def exchange(x, axes):
    return lax.all_to_all(x, axes, 0, 0, tiled=True)


def gather(x, axes):
    n = lax.axis_size(axes)
    return exchange(jnp.broadcast_to(x[None], (n,) + x.shape), axes).reshape(n * x.shape[0], x.shape[1])


def shift(x, axis, d):
    n = lax.axis_size(axis)
    return lax.ppermute(x, axis, [(s, (s + d) % n) for s in range(n)])


def ring_scatter(x, axis):
    n = lax.axis_size(axis)
    me = lax.axis_index(axis)
    blocks = x.reshape(n, x.shape[0] // n, x.shape[1])
    take = lambda d: lax.dynamic_index_in_dim(blocks, lax.rem(me + d, n), 0, keepdims=False)
    arrived = [shift(take(d), axis, d) for d in range(1, n)]
    return sum(arrived, take(0))


def ring_sum(x, axis):
    return sum([shift(x, axis, d) for d in range(1, lax.axis_size(axis))], x)


def ring_gather(x, axis):
    return [x] + [shift(x, axis, d) for d in range(1, lax.axis_size(axis))]


def pair(x, axis, d):
    return lax.ppermute(x, axis, [(s, s ^ d) for s in range(lax.axis_size(axis))])


def quad_gather(x, axis):
    return [x] + [pair(x, axis, d) for d in (1, 2, 3)]


def ordered(parts, me):
    odd = lax.rem(me, 2) == 1
    low = [jnp.where(odd, parts[1], parts[0]), jnp.where(odd, parts[0], parts[1])]
    high = [jnp.where(odd, parts[3], parts[2]), jnp.where(odd, parts[2], parts[3])]
    up = me >= 2
    first = [jnp.where(up, h, l) for l, h in zip(low, high)]
    last = [jnp.where(up, l, h) for l, h in zip(low, high)]
    return jnp.concatenate(first + last, axis=0)


def keep(x, bit):
    half = x.shape[0] // 2
    low, high = x[:half], x[half:]
    return jnp.where(bit == 0, low, high), jnp.where(bit == 0, high, low)


def join(mine, theirs, bit):
    return jnp.where(
        bit == 0, jnp.concatenate([mine, theirs], 0), jnp.concatenate([theirs, mine], 0)
    )


def narrow_places():
    me = lax.axis_index("y")
    return [(lax.rem(me + 4 - d, 4),) for d in range(4)]


def wide_places():
    me = lax.axis_index("x")
    ring = [lax.rem(me + 4 - d, 4) for d in range(4)]
    return [(r, r + 4) for r in ring]


def on_device(tensor, first_factor, third_factor):
    window, second_local, third_local = tensor.shape
    second_total = second_local * lax.axis_size(WIDE)
    third_total = third_local * lax.axis_size(NARROW)
    core = lax.axis_index("core")
    first_wide = first_factor.astype(jnp.float32)
    first_second = first_wide / math.sqrt(window * third_total)
    first_third = first_wide / math.sqrt(window * second_total)
    gram_first = jnp.dot(first_factor.T, first_factor, preferred_element_type=jnp.float32) / window

    gram_part = jnp.dot(third_factor.T, third_factor, preferred_element_type=jnp.float32)
    gram_part = ring_scatter(gram_part, "y")
    gram_part = ring_sum(gram_part, "zh")
    parts = ring_gather(gram_part, "y")
    inverse_second = inverse(parts, narrow_places, gram_first, third_total)

    contracted = jnp.einsum("ijk,kr->ijr", tensor, third_factor, preferred_element_type=jnp.float32)
    partial_second = jnp.sum(contracted * first_second[:, None, :], axis=0)
    row = ring_scatter(partial_second, "y")
    row = ring_sum(row, "zh")
    row = jnp.dot(row, inverse_second, precision=HIGHEST).astype(jnp.bfloat16)
    second_factor = ordered(quad_gather(row, "y"), lax.axis_index("y"))

    first_third, tensor = lax.optimization_barrier((first_third, tensor))
    gram_local = jnp.dot(second_factor.T, second_factor, preferred_element_type=jnp.float32)
    mine, other = keep(gram_local, core)
    mine = mine + shift(other, "core", 1)
    mine = ring_scatter(mine, "x")
    mine = ring_sum(mine, "zl")
    mine = join(mine, shift(mine, "core", 1), core)
    parts = ring_gather(mine, "x")
    inverse_third = inverse(parts, wide_places, gram_first, second_total)

    middle = jnp.einsum("ijk,jr->ikr", tensor, second_factor, preferred_element_type=jnp.float32)
    partial_third = jnp.sum(middle * first_third[:, None, :], axis=0)
    mine, other = keep(partial_third, core)
    mine = mine + shift(other, "core", 1)
    mine = ring_scatter(mine, "x")
    mttkrp_third = ring_scatter(mine, "zl")
    third_solution = jnp.dot(mttkrp_third, inverse_third, precision=HIGHEST)
    mine = gather(third_solution.astype(jnp.bfloat16), CHIP)
    third_new = join(mine, shift(mine, "core", 1), core)

    back = jnp.einsum("ijk,kr->ijr", tensor, third_new, preferred_element_type=jnp.float32)
    partial_first = jnp.sum(back * second_factor.astype(jnp.float32)[None], axis=1)
    partial_first = partial_first + shift(partial_first, "core", 1)
    scale = 1.0 / math.sqrt(second_total * third_total)
    partial_first = (ring_sum(partial_first, "x") * scale).astype(jnp.bfloat16)
    axes = ("zl",) + NARROW
    n = lax.axis_size(axes)
    copies = jnp.broadcast_to(partial_first[None], (n,) + partial_first.shape)
    first_mode = jnp.sum(exchange(copies, axes), axis=0, dtype=jnp.float32)
    return (second_factor, third_new, first_mode)


def solution(mesh):
    fine = Mesh(mesh.devices.reshape(4, 4, 2, 2, 4), WIDE + NARROW)
    in_specs = (P(None, WIDE, NARROW), P(), P(NARROW, None))
    out_specs = (P(WIDE, None), P(NARROW, None), P())
    return jax.shard_map(
        on_device, mesh=fine, in_specs=in_specs, out_specs=out_specs, check_vma=False
    )
```

```python
import functools
import math

import jax
import jax.numpy as jnp
from jax import lax
from jax.experimental import pallas as pl
from jax.experimental.pallas import tpu as pltpu
from jax.sharding import Mesh, PartitionSpec as P

ridge = 0.5
B = 16
WIDE = ("x", "zl", "core")
NARROW = ("zh", "y")
HIGHEST = lax.Precision.HIGHEST


def pieces(x):
    high = x.astype(jnp.bfloat16)
    rest = x - high.astype(jnp.float32)
    middle = rest.astype(jnp.bfloat16)
    low = (rest - middle.astype(jnp.float32)).astype(jnp.bfloat16)
    return high, middle, low


def split_pair(a, b):
    ah, am, al = pieces(a)
    bh, bm, bl = pieces(b)
    left = jnp.concatenate([ah, ah, am, ah, al, am], axis=0)
    return left, jnp.concatenate([bh, bm, bh, bl, bh, bm], axis=0)


def cross(a, b, **kw):
    return lax.dot_general(
        a, b, (((0,), (0,)), ((), ())), preferred_element_type=jnp.float32, **kw
    )


def inverse_kernel(places, total, *refs):
    part_refs, (f_ref, x_ref, m_ref, w_ref) = refs[:-4], refs[-4:]
    n = f_ref.shape[0]
    blocks = [(ref, t, len(group), place) for ref, group in zip(part_refs, places()) for t, place in enumerate(group)]
    for part_ref, t, count, place in blocks:
        depth = part_ref.shape[0] // count
        base = pl.multiple_of(place * depth, depth)
        here = (depth, n)
        diagonal = lax.broadcasted_iota(jnp.int32, here, 0) + base == lax.broadcasted_iota(jnp.int32, here, 1)
        m_ref[pl.ds(base, depth), :] = f_ref[pl.ds(base, depth), :] * (
            part_ref[t * depth:(t + 1) * depth, :] * (1.0 / total)
        ) + jnp.where(diagonal, ridge, 0.0)
    row = lax.broadcasted_iota(jnp.int32, (B, n), 0)
    lane = lax.broadcasted_iota(jnp.int32, (B, n), 1)
    half_row = lax.broadcasted_iota(jnp.int32, (B, 128), 0)
    whole_row = lax.broadcasted_iota(jnp.int32, (n, n), 0)
    whole_lane = lax.broadcasted_iota(jnp.int32, (n, n), 1)

    def step(k, carry):
        panel, left, right = carry
        o = pl.multiple_of(k * B, B)
        cleared = (whole_row >= o) & (whole_lane >= o - B) & (whole_lane < o)
        m_ref[...] = jnp.where(cleared, 0.0, m_ref[...]) - cross(left, right)
        front = pltpu.roll(panel, n - o, 1)
        cols = [jnp.broadcast_to(front[:, j:j + 1], (B, 128)) for j in range(B)]
        inside = (lane >= o) & (lane < o + B)
        unit = jnp.where(lane - o == row, 1.0, 0.0)
        work = jnp.where(inside, unit, panel)
        parts = [work[:, t * 128:(t + 1) * 128] for t in range(n // 128)]
        for j in range(B):
            col = cols[j]
            scale = 1.0 / col[j:j + 1, :]
            other = half_row != j
            for t in range(len(parts)):
                pivot = parts[t][j:j + 1, :] * scale
                parts[t] = jnp.where(other, parts[t] - col * pivot, pivot)
            for m in range(j + 1, B):
                pivot = cols[m][j:j + 1, :] * scale
                cols[m] = jnp.where(other, cols[m] - col * pivot, pivot)
        solved = jnp.concatenate(parts, axis=1)
        left, right = split_pair(jnp.where(lane >= o + B, panel, 0.0), solved)
        ahead = split_pair(front[:, :128], front[:, :128])[0][:, B:2 * B]
        following = pl.multiple_of(jnp.minimum(o + B, n - B), B)
        panel_next = jnp.where(inside, 0.0, m_ref[pl.ds(following, B), :]) - cross(ahead, right)
        m_ref[pl.ds(o, B), :] = jnp.where(lane < o, panel, jnp.where(inside, unit, 0.0))
        w_ref[pl.ds(o, B), :] = jnp.where(lane < o + B, solved, 0.0)
        return panel_next, left, right

    nothing = jnp.zeros((6 * B, n), jnp.bfloat16)
    lax.fori_loop(0, n // B, step, (m_ref[0:B, :], nothing, nothing))
    x_ref[...] = cross(m_ref[...], w_ref[...], precision=HIGHEST)


def inverse(parts, places, gram_first, total):
    n = gram_first.shape[0]
    return pl.pallas_call(
        functools.partial(inverse_kernel, places, total),
        out_shape=jax.ShapeDtypeStruct((n, n), jnp.float32),
        in_specs=[pl.BlockSpec(memory_space=pltpu.VMEM)] * (len(parts) + 1),
        out_specs=pl.BlockSpec(memory_space=pltpu.VMEM),
        scratch_shapes=[pltpu.VMEM((n, n), jnp.float32), pltpu.VMEM((n, n), jnp.float32)],
        cost_estimate=pl.CostEstimate(flops=6 * 2 * n**3, bytes_accessed=8 * n * n, transcendentals=0),
        compiler_params=pltpu.CompilerParams(vmem_limit_bytes=8 << 20),
        name="inverse",
    )(*parts, gram_first)


def exchange(x, axes):
    return lax.all_to_all(x, axes, 0, 0, tiled=True)


def shift(x, axis, d):
    n = lax.axis_size(axis)
    return lax.ppermute(x, axis, [(s, (s + d) % n) for s in range(n)])


def ring_scatter(x, axis):
    n = lax.axis_size(axis)
    me = lax.axis_index(axis)
    blocks = x.reshape(n, x.shape[0] // n, x.shape[1])
    own, *sent = [
        lax.dynamic_index_in_dim(blocks, lax.rem(me + d, n), 0, keepdims=False) for d in range(n)
    ]
    arrived = [shift(block, axis, d + 1) for d, block in enumerate(sent)]
    return sum(arrived, own)


def ring_sum(x, axis):
    return sum([shift(x, axis, d) for d in range(1, lax.axis_size(axis))], x)


def ring_gather(x, axis):
    return [x] + [shift(x, axis, d) for d in range(1, lax.axis_size(axis))]


def pair(x, axis, d):
    return lax.ppermute(x, axis, [(s, s ^ d) for s in range(lax.axis_size(axis))])


def quad_gather(x, axis):
    return [x] + [pair(x, axis, d) for d in (1, 2, 3)]


def ordered(parts, me):
    odd = lax.rem(me, 2) == 1
    low = [jnp.where(odd, parts[1], parts[0]), jnp.where(odd, parts[0], parts[1])]
    high = [jnp.where(odd, parts[3], parts[2]), jnp.where(odd, parts[2], parts[3])]
    up = me >= 2
    first = [jnp.where(up, h, l) for l, h in zip(low, high)]
    last = [jnp.where(up, l, h) for l, h in zip(low, high)]
    return jnp.concatenate(first + last, axis=0)


def keep(x, bit):
    half = x.shape[0] // 2
    low, high = x[:half], x[half:]
    return jnp.where(bit == 0, low, high), jnp.where(bit == 0, high, low)


def join(mine, theirs, bit):
    return jnp.where(
        bit == 0, jnp.concatenate([mine, theirs], 0), jnp.concatenate([theirs, mine], 0)
    )


def narrow_places():
    me = lax.axis_index("y")
    return [(lax.rem(me + 4 - d, 4),) for d in range(4)]


def wide_places():
    me = lax.axis_index("x")
    ring = [lax.rem(me + 4 - d, 4) for d in range(4)]
    return [(r, r + 4) for r in ring]


def on_device(tensor, first_factor, third_factor):
    window, second_local, third_local = tensor.shape
    second_total = second_local * lax.axis_size(WIDE)
    third_total = third_local * lax.axis_size(NARROW)
    core = lax.axis_index("core")
    first_wide = first_factor.astype(jnp.float32)
    first_second = first_wide / math.sqrt(window * third_total)
    first_third = first_wide / math.sqrt(window * second_total)
    gram_first = jnp.dot(first_factor.T, first_factor, preferred_element_type=jnp.float32) / window

    gram_part = jnp.dot(third_factor.T, third_factor, preferred_element_type=jnp.float32)
    gram_part = ring_scatter(gram_part, "y")
    gram_part = ring_sum(gram_part, "zh")
    parts = ring_gather(gram_part, "y")
    inverse_second = inverse(parts, narrow_places, gram_first, third_total)

    contracted = jnp.einsum("ijk,kr->ijr", tensor, third_factor, preferred_element_type=jnp.float32)
    partial_second = jnp.sum(contracted * first_second[:, None, :], axis=0)
    row = ring_scatter(partial_second, "y")
    row = ring_sum(row, "zh")
    row = jnp.dot(row, inverse_second, precision=HIGHEST).astype(jnp.bfloat16)
    second_factor = ordered(quad_gather(row, "y"), lax.axis_index("y"))

    first_third, tensor = lax.optimization_barrier((first_third, tensor))
    gram_local = jnp.dot(second_factor.T, second_factor, preferred_element_type=jnp.float32)
    mine, other = keep(gram_local, core)
    mine = mine + shift(other, "core", 1)
    mine = ring_scatter(mine, "x")
    mine = ring_sum(mine, "zl")
    mine = join(mine, shift(mine, "core", 1), core)
    parts = ring_gather(mine, "x")
    inverse_third = inverse(parts, wide_places, gram_first, second_total)

    middle = jnp.einsum("ijk,jr->ikr", tensor, second_factor, preferred_element_type=jnp.float32)
    partial_third = jnp.sum(middle * first_third[:, None, :], axis=0)
    mine, other = keep(partial_third, core)
    mine = mine + shift(other, "core", 1)
    mine = ring_scatter(mine, "x")
    mttkrp_third = ring_sum(mine, "zl")
    third_solution = jnp.dot(mttkrp_third, inverse_third, precision=HIGHEST)
    block = third_solution.astype(jnp.bfloat16)
    copies = jnp.broadcast_to(block[None], (lax.axis_size("x"),) + block.shape)
    mine = exchange(copies, "x").reshape(-1, block.shape[1])
    third_new = join(mine, shift(mine, "core", 1), core)

    back = jnp.einsum("ijk,kr->ijr", tensor, third_new, preferred_element_type=jnp.float32)
    partial_first = jnp.sum(back * second_factor.astype(jnp.float32)[None], axis=1)
    partial_first = partial_first + shift(partial_first, "core", 1)
    scale = 1.0 / math.sqrt(second_total * third_total)
    partial_first = (ring_sum(partial_first, "x") * scale).astype(jnp.bfloat16)
    axes = ("zl",) + NARROW
    n = lax.axis_size(axes)
    copies = jnp.broadcast_to(partial_first[None], (n,) + partial_first.shape)
    first_mode = jnp.sum(exchange(copies, axes), axis=0, dtype=jnp.float32)
    return (second_factor, third_new, first_mode)


def solution(mesh):
    fine = Mesh(mesh.devices.reshape(4, 4, 2, 2, 4), WIDE + NARROW)
    in_specs = (P(None, WIDE, NARROW), P(), P(NARROW, None))
    out_specs = (P(WIDE, None), P(NARROW, None), P())
    return jax.shard_map(
        on_device, mesh=fine, in_specs=in_specs, out_specs=out_specs, check_vma=False
    )
```

```python
import functools
import math

import jax
import jax.numpy as jnp
from jax import lax
from jax.experimental import pallas as pl
from jax.experimental.pallas import tpu as pltpu
from jax.sharding import Mesh, PartitionSpec as P

ridge = 0.5
B = 16
WIDE = ("x", "zl", "core")
NARROW = ("zh", "y")
HIGHEST = lax.Precision.HIGHEST


def pieces(x):
    high = x.astype(jnp.bfloat16)
    rest = x - high.astype(jnp.float32)
    middle = rest.astype(jnp.bfloat16)
    low = (rest - middle.astype(jnp.float32)).astype(jnp.bfloat16)
    return high, middle, low


def split_pair(a, b):
    ah, am, al = pieces(a)
    bh, bm, bl = pieces(b)
    left = jnp.concatenate([ah, ah, am, ah, al, am], axis=0)
    return left, jnp.concatenate([bh, bm, bh, bl, bh, bm], axis=0)


def cross(a, b, **kw):
    return lax.dot_general(
        a, b, (((0,), (0,)), ((), ())), preferred_element_type=jnp.float32, **kw
    )


def inverse_kernel(places, total, *refs):
    part_refs, (f_ref, x_ref, m_ref, w_ref) = refs[:-4], refs[-4:]
    n = f_ref.shape[0]
    blocks = [(ref, t, len(group), place) for ref, group in zip(part_refs, places()) for t, place in enumerate(group)]
    for part_ref, t, count, place in blocks:
        depth = part_ref.shape[0] // count
        base = pl.multiple_of(place * depth, depth)
        here = (depth, n)
        diagonal = lax.broadcasted_iota(jnp.int32, here, 0) + base == lax.broadcasted_iota(jnp.int32, here, 1)
        m_ref[pl.ds(base, depth), :] = f_ref[pl.ds(base, depth), :] * (
            part_ref[t * depth:(t + 1) * depth, :] * (1.0 / total)
        ) + jnp.where(diagonal, ridge, 0.0)
    row = lax.broadcasted_iota(jnp.int32, (B, n), 0)
    lane = lax.broadcasted_iota(jnp.int32, (B, n), 1)
    half_row = lax.broadcasted_iota(jnp.int32, (B, 128), 0)
    whole_row = lax.broadcasted_iota(jnp.int32, (n, n), 0)
    whole_lane = lax.broadcasted_iota(jnp.int32, (n, n), 1)

    def step(k, carry):
        panel, left, right = carry
        o = pl.multiple_of(k * B, B)
        cleared = (whole_row >= o) & (whole_lane >= o - B) & (whole_lane < o)
        m_ref[...] = jnp.where(cleared, 0.0, m_ref[...]) - cross(left, right)
        front = pltpu.roll(panel, n - o, 1)
        cols = [jnp.broadcast_to(front[:, j:j + 1], (B, 128)) for j in range(B)]
        inside = (lane >= o) & (lane < o + B)
        unit = jnp.where(lane - o == row, 1.0, 0.0)
        work = jnp.where(inside, unit, panel)
        parts = [work[:, t * 128:(t + 1) * 128] for t in range(n // 128)]
        for j in range(B):
            col = cols[j]
            scale = 1.0 / col[j:j + 1, :]
            other = half_row != j
            for t in range(len(parts)):
                pivot = parts[t][j:j + 1, :] * scale
                parts[t] = jnp.where(other, parts[t] - col * pivot, pivot)
            for m in range(j + 1, B):
                pivot = cols[m][j:j + 1, :] * scale
                cols[m] = jnp.where(other, cols[m] - col * pivot, pivot)
        solved = jnp.concatenate(parts, axis=1)
        left, right = split_pair(jnp.where(lane >= o + B, panel, 0.0), solved)
        ahead = split_pair(front[:, :128], front[:, :128])[0][:, B:2 * B]
        following = pl.multiple_of(jnp.minimum(o + B, n - B), B)
        panel_next = jnp.where(inside, 0.0, m_ref[pl.ds(following, B), :]) - cross(ahead, right)
        m_ref[pl.ds(o, B), :] = jnp.where(lane < o, panel, jnp.where(inside, unit, 0.0))
        w_ref[pl.ds(o, B), :] = jnp.where(lane < o + B, solved, 0.0)
        return panel_next, left, right

    nothing = jnp.zeros((6 * B, n), jnp.bfloat16)
    lax.fori_loop(0, n // B, step, (m_ref[0:B, :], nothing, nothing))

    def finish(h, carry):
        here = pl.ds(pl.multiple_of(h * 128, 128), 128)
        x_ref[here, :] = cross(m_ref[:, here], w_ref[...], precision=HIGHEST)
        return carry

    lax.fori_loop(0, n // 128, finish, 0)


def inverse(parts, places, gram_first, total):
    n = gram_first.shape[0]
    return pl.pallas_call(
        functools.partial(inverse_kernel, places, total),
        out_shape=jax.ShapeDtypeStruct((n, n), jnp.float32),
        in_specs=[pl.BlockSpec(memory_space=pltpu.VMEM)] * (len(parts) + 1),
        out_specs=pl.BlockSpec(memory_space=pltpu.VMEM),
        scratch_shapes=[pltpu.VMEM((n, n), jnp.float32), pltpu.VMEM((n, n), jnp.float32)],
        cost_estimate=pl.CostEstimate(flops=6 * 2 * n**3, bytes_accessed=8 * n * n, transcendentals=0),
        compiler_params=pltpu.CompilerParams(vmem_limit_bytes=8 << 20),
        name="inverse",
    )(*parts, gram_first)


def exchange(x, axes):
    return lax.all_to_all(x, axes, 0, 0, tiled=True)


def shift(x, axis, d):
    n = lax.axis_size(axis)
    return lax.ppermute(x, axis, [(s, (s + d) % n) for s in range(n)])


def ring_scatter(x, axis):
    n = lax.axis_size(axis)
    me = lax.axis_index(axis)
    blocks = x.reshape(n, x.shape[0] // n, x.shape[1])
    own, *sent = [
        lax.dynamic_index_in_dim(blocks, lax.rem(me + d, n), 0, keepdims=False) for d in range(n)
    ]
    arrived = [shift(block, axis, d + 1) for d, block in enumerate(sent)]
    return sum(arrived, own)


def ring_sum(x, axis):
    return sum([shift(x, axis, d) for d in range(1, lax.axis_size(axis))], x)


def ring_gather(x, axis):
    return [x] + [shift(x, axis, d) for d in range(1, lax.axis_size(axis))]


def pair(x, axis, d):
    return lax.ppermute(x, axis, [(s, s ^ d) for s in range(lax.axis_size(axis))])


def quad_gather(x, axis):
    return [x] + [pair(x, axis, d) for d in (1, 2, 3)]


def ordered(parts, me):
    rows = parts[0].shape[0]
    whole = jnp.zeros((len(parts) * rows, parts[0].shape[1]), parts[0].dtype)
    for d, part in enumerate(parts):
        whole = lax.dynamic_update_slice(whole, part, (jnp.bitwise_xor(me, d) * rows, 0))
    return whole


def sorted_rows(parts, me):
    odd = lax.rem(me, 2) == 1
    low = [jnp.where(odd, parts[1], parts[0]), jnp.where(odd, parts[0], parts[1])]
    high = [jnp.where(odd, parts[3], parts[2]), jnp.where(odd, parts[2], parts[3])]
    up = me >= 2
    first = [jnp.where(up, h, l) for l, h in zip(low, high)]
    last = [jnp.where(up, l, h) for l, h in zip(low, high)]
    return jnp.concatenate(first + last, axis=0)


def keep(x, bit):
    half = x.shape[0] // 2
    low, high = x[:half], x[half:]
    return jnp.where(bit == 0, low, high), jnp.where(bit == 0, high, low)


def join(mine, theirs, bit):
    return jnp.where(
        bit == 0, jnp.concatenate([mine, theirs], 0), jnp.concatenate([theirs, mine], 0)
    )


def narrow_places():
    me = lax.axis_index("y")
    return [(lax.rem(me + 4 - d, 4),) for d in range(4)]


def wide_places():
    me = lax.axis_index("x")
    ring = [lax.rem(me + 4 - d, 4) for d in range(4)]
    return [(r, r + 4) for r in ring]


def on_device(tensor, first_factor, third_factor):
    window, second_local, third_local = tensor.shape
    second_total = second_local * lax.axis_size(WIDE)
    third_total = third_local * lax.axis_size(NARROW)
    core = lax.axis_index("core")
    first_wide = first_factor.astype(jnp.float32)
    first_second = first_wide / math.sqrt(window * third_total)
    first_third = first_wide / math.sqrt(window * second_total)
    gram_first = jnp.dot(first_factor.T, first_factor, preferred_element_type=jnp.float32) / window

    gram_part = jnp.dot(third_factor.T, third_factor, preferred_element_type=jnp.float32)
    gram_part = ring_scatter(gram_part, "y")
    gram_part = ring_sum(gram_part, "zh")
    parts = ring_gather(gram_part, "y")
    inverse_second = inverse(parts, narrow_places, gram_first, third_total)

    contracted = jnp.einsum("ijk,kr->ijr", tensor, third_factor, preferred_element_type=jnp.float32)
    partial_second = jnp.sum(contracted * first_second[:, None, :], axis=0)
    row = ring_scatter(partial_second, "y")
    row = ring_sum(row, "zh")
    row = jnp.dot(row, inverse_second, precision=HIGHEST).astype(jnp.bfloat16)
    second_factor = sorted_rows(quad_gather(row, "y"), lax.axis_index("y"))

    first_third, tensor = lax.optimization_barrier((first_third, tensor))
    gram_local = jnp.dot(second_factor.T, second_factor, preferred_element_type=jnp.float32)
    mine, other = keep(gram_local, core)
    mine = mine + shift(other, "core", 1)
    mine = ring_scatter(mine, "x")
    mine = ring_sum(mine, "zl")
    mine = join(mine, shift(mine, "core", 1), core)
    parts = ring_gather(mine, "x")
    inverse_third = inverse(parts, wide_places, gram_first, second_total)

    middle = jnp.einsum("ijk,jr->ikr", tensor, second_factor, preferred_element_type=jnp.float32)
    partial_third = jnp.sum(middle * first_third[:, None, :], axis=0)
    mine, other = keep(partial_third, core)
    mine = mine + shift(other, "core", 1)
    mine = ring_scatter(mine, "x")
    mttkrp_third = ring_sum(mine, "zl")
    third_solution = jnp.dot(mttkrp_third, inverse_third, precision=HIGHEST)
    mine = ordered(quad_gather(third_solution.astype(jnp.bfloat16), "x"), lax.axis_index("x"))
    third_new = ordered([mine, shift(mine, "core", 1)], core)

    back = jnp.einsum("ijk,kr->ijr", tensor, third_new, preferred_element_type=jnp.float32)
    partial_first = jnp.sum(back * second_factor.astype(jnp.float32)[None], axis=1)
    partial_first = partial_first + shift(partial_first, "core", 1)
    scale = 1.0 / math.sqrt(second_total * third_total)
    partial_first = (ring_sum(partial_first, "x") * scale).astype(jnp.bfloat16)
    axes = ("zl",) + NARROW
    n = lax.axis_size(axes)
    copies = jnp.broadcast_to(partial_first[None], (n,) + partial_first.shape)
    first_mode = jnp.sum(exchange(copies, axes), axis=0, dtype=jnp.float32)
    return (second_factor, third_new, first_mode)


def solution(mesh):
    fine = Mesh(mesh.devices.reshape(4, 4, 2, 2, 4), WIDE + NARROW)
    in_specs = (P(None, WIDE, NARROW), P(), P(NARROW, None))
    out_specs = (P(WIDE, None), P(NARROW, None), P())
    return jax.shard_map(
        on_device, mesh=fine, in_specs=in_specs, out_specs=out_specs, check_vma=False
    )
```
